32 devices in a mesh: grp: 16 (over z, y, x), lag: 2 (over core).
Axes of the slice: x: 2, y: 2, z: 4, core: 2. Of those that a mesh axis runs over, the one named last changes fastest.
Arguments:
- waveforms: float32 [256, 8, 2048], P('grp'), may hold values from -6 to 6
- pair_bin: int32 [256, 256], P('grp'), may hold values from 0 to 127, as said below
Outputs:
- stack: float32 [128, 1024], P('grp', 'lag')
The draws below stay inside these ranges and needn't reach their ends.
Inputs may be any that keep to these rules, and one draw needn't show every extreme that they name: pair_bin is symmetric: the bin of stations i and j is that of j and i.
All inputs are finite; a program needn't handle non-finite values.
Results may differ from the reference program's by a relative error of at most 0.0049.
Values may be sent and summed in bfloat16 or wider, within the bound.
No kernel may reach another device: no remote copies, remote signals or barrier semaphores. Data moves between devices by JAX's collectives and lax.ppermute only.
A program may use at most 64 MiB of HBM per device.

```python
import math
import jax
import jax.numpy as jnp
from jax import lax

STA_DEV = 16
SEG = 8
NFFT = 2048
LAGS = 1024
HW = 32
STATIONS = 256
BINS = 128


def draw_pair_bin(key, part):
    raw_bins = jax.random.randint(key, (STATIONS, STATIONS), 0, BINS, dtype=jnp.int32)
    row_index = jnp.arange(STATIONS, dtype=jnp.int32)[:, None]
    column_index = jnp.arange(STATIONS, dtype=jnp.int32)[None, :]
    return jnp.where(row_index < column_index, raw_bins, raw_bins.T)


def levels(key, extent, pieces, smallest, largest):
    def one(dim, parts):
        heights = jax.random.uniform(jax.random.fold_in(jax.random.fold_in(key, 6), dim), (parts,), jnp.float32, smallest / len(pieces), largest / len(pieces))
        return jnp.repeat(jnp.exp(heights), extent[dim] // parts).reshape((-1,) + (1,) * (len(extent) - dim - 1))

    gain = one(*pieces[0])
    for cut in pieces[1:]:
        gain = gain * one(*cut)
    return gain


def gaussian(rng, dims, scale, most, cuts=(), kind=jnp.bfloat16):
    level = levels(rng, dims, cuts, -0.22, 0.18) if cuts else 1.0
    drawn = jax.random.normal(rng, dims, jnp.float32) * scale * level
    return jnp.minimum(jnp.maximum(drawn, -most), most).astype(kind)


def setup_inputs(seed: int = 0) -> dict:
    streams_of = jax.random.split(jax.random.key(seed), 3)
    return {
        "waveforms": gaussian(streams_of[0], (STATIONS, SEG, NFFT), 1.0, 6.0, ((0, 16),), jnp.float32),
        "pair_bin": draw_pair_bin(jax.random.fold_in(streams_of[2], 71), 0),
    }


EPSILON = 1e-06

def forward_table(freq_start, freq_count):
    sample_index = jnp.arange(NFFT, dtype=jnp.int32)[:, None]
    bin_index = freq_start + jnp.arange(freq_count, dtype=jnp.int32)[None, :]
    phase = (sample_index * bin_index % NFFT).astype(jnp.float32) * (2.0 * math.pi / NFFT)
    return jnp.concatenate([jnp.cos(phase), -jnp.sin(phase)], axis=1)

def inverse_table(freq_start, freq_count):
    bin_index = freq_start + jnp.arange(freq_count, dtype=jnp.int32)
    shifted = jnp.arange(LAGS, dtype=jnp.int32) - LAGS // 2
    phase = (bin_index[:, None] * shifted[None, :] % NFFT).astype(jnp.float32) * (2.0 * math.pi / NFFT)
    weight = jnp.where(bin_index == 0, 1.0, 2.0).astype(jnp.float32)[:, None] / NFFT
    return jnp.concatenate([weight * jnp.cos(phase), -weight * jnp.sin(phase)], axis=0)

def window_band(freq_count):
    padded_index = jnp.arange(freq_count + 2 * HW, dtype=jnp.int32)[:, None]
    bin_index = jnp.arange(freq_count, dtype=jnp.int32)[None, :]
    inside = (padded_index >= bin_index) & (padded_index <= bin_index + 2 * HW)
    return inside.astype(jnp.float32)

def window_count(freq_start, freq_count, half_length):
    bin_index = freq_start + jnp.arange(freq_count, dtype=jnp.int32)
    upper = jnp.minimum(bin_index + HW, half_length - 1)
    lower = jnp.maximum(bin_index - HW, 0)
    return (upper - lower + 1).astype(jnp.float32)

def reference(waveforms, pair_bin):
    station_total = waveforms.shape[0]
    half_length = NFFT // 2
    spectra = jnp.dot(waveforms.reshape(station_total * SEG, NFFT), forward_table(0, half_length), precision=lax.Precision.HIGHEST, preferred_element_type=jnp.float32)
    spectra = spectra.reshape(station_total, SEG, 2 * half_length)
    real_part = spectra[..., :half_length]
    imag_part = spectra[..., half_length:]
    amplitude = jnp.sqrt(real_part * real_part + imag_part * imag_part)
    padded = jnp.pad(amplitude, ((0, 0), (0, 0), (HW, HW)))
    smoothed = jnp.dot(padded.reshape(station_total * SEG, half_length + 2 * HW), window_band(half_length), precision=lax.Precision.HIGHEST, preferred_element_type=jnp.float32)
    smoothed = smoothed.reshape(station_total, SEG, half_length) / window_count(0, half_length, half_length)
    whitened = jnp.concatenate([real_part / (smoothed + EPSILON), imag_part / (smoothed + EPSILON)], axis=2).astype(jnp.bfloat16)
    all_real = whitened[..., :half_length].astype(jnp.float32)
    all_imag = whitened[..., half_length:].astype(jnp.float32)
    far_stack = jnp.concatenate([all_real, all_imag], axis=1)
    far_alt = jnp.concatenate([all_imag, all_real], axis=1)
    group_count = station_total // STA_DEV
    grouped = whitened.reshape(group_count, STA_DEV, SEG, 2 * half_length)
    bin_rows = pair_bin.reshape(group_count, STA_DEV, station_total)
    column_index = jnp.arange(station_total, dtype=jnp.int32)

    def add_group(running, inputs):
        rows, row_bins, group_index = inputs
        own_real = rows[..., :half_length].astype(jnp.float32)
        own_imag = rows[..., half_length:].astype(jnp.float32)
        own_stack = jnp.concatenate([own_real, own_imag], axis=1)
        own_alt = jnp.concatenate([own_real, -own_imag], axis=1)
        real_sum = jnp.einsum('asf,bsf->abf', own_stack, far_stack)
        imag_sum = jnp.einsum('asf,bsf->abf', own_alt, far_alt)
        cross = jnp.concatenate([real_sum, imag_sum], axis=2).astype(jnp.bfloat16)
        cross = lax.optimization_barrier(cross).astype(jnp.float32)
        row_index = group_index * STA_DEV + jnp.arange(STA_DEV, dtype=jnp.int32)
        segment_ids = jnp.where(column_index[None, :] > row_index[:, None], row_bins, BINS).reshape(-1)
        summed = jax.ops.segment_sum(cross.reshape(STA_DEV * station_total, 2 * half_length), segment_ids, num_segments=BINS + 1)
        return (running + summed[:BINS], None)
    initial = jnp.zeros((BINS, 2 * half_length), jnp.float32)
    binned, _ = lax.scan(add_group, initial, (grouped, bin_rows, jnp.arange(group_count, dtype=jnp.int32)))
    return jnp.dot(binned, inverse_table(0, half_length), precision=lax.Precision.HIGHEST, preferred_element_type=jnp.float32)
```

```python
import math

import jax
import jax.numpy as jnp
import ml_dtypes
import numpy as np
from jax import lax
from jax.experimental import pallas as pl
from jax.experimental.pallas import tpu as pltpu
from jax.sharding import PartitionSpec as P

NFFT = 2048
LAGS = 1024
HW = 32
BIN_DEV = 8


EPSILON = 1e-06


def with_halo(block, sides, width):
    for axis, dim in sides:
        count = lax.axis_size(axis)
        forward = [(i, i + 1) for i in range(count - 1)]
        backward = [(target, source) for source, target in forward]
        low = lax.ppermute(
            lax.slice_in_dim(block, block.shape[dim] - width, None, axis=dim), axis, forward
        )
        high = lax.ppermute(lax.slice_in_dim(block, 0, width, axis=dim), axis, backward)
        block = jnp.concatenate([low, block, high], axis=dim)
    return block


def forward_table(freq_start, freq_count):
    sample_index = jnp.arange(NFFT, dtype=jnp.int32)[:, None]
    bin_index = freq_start + jnp.arange(freq_count, dtype=jnp.int32)[None, :]
    phase = (sample_index * bin_index % NFFT).astype(jnp.float32) * (2.0 * math.pi / NFFT)
    return jnp.concatenate([jnp.cos(phase), -jnp.sin(phase)], axis=1)


def inverse_table(freq_start, freq_count):
    bin_index = freq_start + jnp.arange(freq_count, dtype=jnp.int32)
    shifted = jnp.arange(LAGS, dtype=jnp.int32) - LAGS // 2
    phase = (bin_index[:, None] * shifted[None, :] % NFFT).astype(jnp.float32) * (
        2.0 * math.pi / NFFT
    )
    weight = jnp.where(bin_index == 0, 1.0, 2.0).astype(jnp.float32)[:, None] / NFFT
    return jnp.concatenate([weight * jnp.cos(phase), -weight * jnp.sin(phase)], axis=0)


def window_band(freq_count):
    padded_index = jnp.arange(freq_count + 2 * HW, dtype=jnp.int32)[:, None]
    bin_index = jnp.arange(freq_count, dtype=jnp.int32)[None, :]
    inside = (padded_index >= bin_index) & (padded_index <= bin_index + 2 * HW)
    return inside.astype(jnp.float32)


def window_count(freq_start, freq_count, half_length):
    bin_index = freq_start + jnp.arange(freq_count, dtype=jnp.int32)
    upper = jnp.minimum(bin_index + HW, half_length - 1)
    lower = jnp.maximum(bin_index - HW, 0)
    return (upper - lower + 1).astype(jnp.float32)


def add_block(running, whitened, remote, column_start, keep_pairs, imag_sign, pair_bin):
    freq_count = whitened.shape[2] // 2
    row_count = whitened.shape[0]
    column_count = remote.shape[0]
    own_real = whitened[..., :freq_count]
    own_imag = whitened[..., freq_count:]
    far_real = remote[..., :freq_count]
    far_imag = remote[..., freq_count:]
    own_stack = jnp.concatenate([own_real, own_imag], axis=1)
    own_alt = jnp.concatenate([own_real, -own_imag], axis=1)
    far_stack = jnp.concatenate([far_real, far_imag], axis=1)
    far_alt = jnp.concatenate([far_imag, far_real], axis=1)
    real_sum = jnp.einsum("asf,bsf->abf", own_stack, far_stack, preferred_element_type=jnp.float32)
    imag_sum = (
        jnp.einsum("asf,bsf->abf", own_alt, far_alt, preferred_element_type=jnp.float32) * imag_sign
    )
    cross = jnp.concatenate([real_sum, imag_sum], axis=2).astype(jnp.bfloat16)
    cross = cross.reshape(row_count * column_count, 2 * freq_count)
    block_bins = lax.dynamic_slice_in_dim(pair_bin, column_start, column_count, 1)
    block_bins = jnp.where(keep_pairs, block_bins, -1).reshape(-1)
    onehot = (block_bins[None, :] == jnp.arange(running.shape[0], dtype=jnp.int32)[:, None]).astype(
        jnp.bfloat16
    )
    return running + jnp.dot(onehot, cross, preferred_element_type=jnp.float32)


def local(waveforms, pair_bin):
    station_count = waveforms.shape[0]
    segments = waveforms.shape[1]
    groups = lax.axis_size("grp")
    group_index = lax.axis_index("grp")
    half_length = NFFT // 2
    freq_count = half_length // lax.axis_size("lag")
    freq_start = lax.axis_index("lag") * freq_count
    spectra = jnp.dot(
        waveforms.reshape(station_count * segments, NFFT),
        forward_table(freq_start, freq_count),
        precision=lax.Precision.HIGHEST,
        preferred_element_type=jnp.float32,
    )
    spectra = spectra.reshape(station_count, segments, 2 * freq_count)
    real_part = spectra[..., :freq_count]
    imag_part = spectra[..., freq_count:]
    amplitude = jnp.sqrt(real_part * real_part + imag_part * imag_part)
    padded = with_halo(amplitude, (("lag", 2),), HW)
    smoothed = jnp.dot(
        padded.reshape(station_count * segments, freq_count + 2 * HW),
        window_band(freq_count),
        precision=lax.Precision.HIGHEST,
        preferred_element_type=jnp.float32,
    )
    smoothed = smoothed.reshape(station_count, segments, freq_count) / window_count(
        freq_start, freq_count, half_length
    )
    whitened = jnp.concatenate(
        [real_part / (smoothed + EPSILON), imag_part / (smoothed + EPSILON)], axis=2
    ).astype(jnp.bfloat16)
    bins_total = BIN_DEV * groups
    row_start = group_index * station_count
    initial = jnp.zeros((bins_total, 2 * freq_count), jnp.float32)
    local_rows = jnp.arange(station_count, dtype=jnp.int32)
    remote = lax.all_gather(whitened, "grp", axis=0, tiled=True)
    group_total = remote.shape[0] // station_count
    per_step = max((divisor for divisor in (4, 3, 2, 1) if group_total % divisor == 0))
    step_count = group_total // per_step
    block_width = per_step * station_count
    blocks = remote.reshape(step_count, block_width, remote.shape[1], remote.shape[2])

    def one_step(step_index, carried):
        column_block = lax.dynamic_index_in_dim(blocks, step_index, 0, keepdims=False)
        column_start = step_index * block_width
        column_index = column_start + jnp.arange(block_width, dtype=jnp.int32)
        keep_pairs = column_index[None, :] > (row_start + local_rows)[:, None]

        def compute(accumulated):
            return add_block(
                accumulated, whitened, column_block, column_start, keep_pairs, 1.0, pair_bin
            )

        return lax.cond(
            column_start + block_width > row_start,
            compute,
            lambda accumulated: accumulated,
            carried,
        )

    binned = lax.fori_loop(0, step_count, one_step, initial)
    inverse = inverse_table(freq_start, freq_count)
    owned_bins = lax.psum_scatter(binned, "grp", scatter_dimension=0, tiled=True)
    lag_partial = jnp.dot(
        owned_bins, inverse, precision=lax.Precision.HIGHEST, preferred_element_type=jnp.float32
    )
    return lax.psum_scatter(lag_partial, "lag", scatter_dimension=1, tiled=True)


LANES = 128
RADIX = 4
SPLIT = NFFT // RADIX
PACK = 16


def halves(table):
    wide = np.asarray(table, np.float32)
    high = wide.astype(ml_dtypes.bfloat16)
    return high, (wide - high.astype(np.float32)).astype(ml_dtypes.bfloat16)


def forward_constants(freq_count, lag_count):
    high, low, halo, band, inverse_count = [], [], [], [], []
    sample = np.arange(SPLIT)
    for index in range(lag_count):
        start = index * freq_count
        order = start + np.concatenate(
            [np.arange(freq_count // RADIX) * RADIX + r for r in range(RADIX)]
        )
        per_class = order.reshape(RADIX, -1)
        angle = 2.0 * np.pi / NFFT * (sample[None, :, None] * per_class[:, None, :] % NFFT)
        table = np.concatenate([np.cos(angle), np.sin(angle)], axis=2)
        table_high, table_low = halves(table)
        high.append(table_high)
        low.append(table_low)
        beyond = np.concatenate(
            [np.arange(start - HW, start), np.arange(start + freq_count, start + freq_count + HW)]
        )
        beyond = beyond[(beyond >= 0) & (beyond < NFFT // 2)]
        angle = 2.0 * np.pi / NFFT * (np.arange(NFFT)[:, None] * beyond[None, :] % NFFT)
        side = np.zeros((NFFT, 2 * LANES))
        side[:, : beyond.size] = np.cos(angle)
        side[:, LANES : LANES + beyond.size] = np.sin(angle)
        halo.append(halves(side)[0])
        near = np.zeros((freq_count + LANES, freq_count))
        seen = np.concatenate([order, beyond])
        near[: seen.size] = np.abs(seen[:, None] - order[None, :]) <= HW
        band.append(near.astype(ml_dtypes.bfloat16))
        upper = np.minimum(order + HW, NFFT // 2 - 1)
        lower = np.maximum(order - HW, 0)
        inverse_count.append((1.0 / (upper - lower + 1))[None, :].astype(np.float32))
    return tuple(np.stack(part) for part in (high, low, halo, band, inverse_count))


def inverse_constants(freq_count, lag_count, groups):
    run = freq_count // groups
    quarter = run // RADIX
    index = np.arange(groups * lag_count)
    start = (index % lag_count) * freq_count + (index // lag_count) * run
    pair, half, step = np.meshgrid(np.arange(2), np.arange(2), np.arange(quarter), indexing="ij")
    offset = (RADIX * step + 2 * pair + half).reshape(2, PACK)
    bins = start[:, None, None] + offset[None]
    both = np.stack([bins, bins], axis=2)
    imaginary = np.stack([np.zeros_like(bins), np.ones_like(bins)], axis=2).reshape(-1)
    both = both.reshape(-1)
    angle = 2.0 * np.pi / NFFT * (both[:, None] * np.arange(LANES)[None, :] % NFFT)
    table = np.where(imaginary[:, None] == 1, -np.sin(angle), np.cos(angle))
    table_high, table_low = halves(table)
    lag_block = LAGS // lag_count
    weight = np.where(both == 0, 1.0, 2.0) / NFFT
    own, swapped = [], []
    for lag in range(lag_count):
        first = np.arange(lag_block // LANES) * LANES + lag * lag_block - LAGS // 2
        angle = 2.0 * np.pi / NFFT * (both[None, :] * first[:, None] % NFFT)
        own.append(weight * np.cos(angle))
        swapped.append(np.where(imaginary == 1, 1.0, -1.0) * weight * np.sin(angle))
    return (
        table_high,
        table_low,
        np.stack(own).astype(np.float32),
        np.stack(swapped).astype(np.float32),
    )


def split_float(value):
    high = value.astype(jnp.bfloat16)
    return high, (value - high.astype(jnp.float32)).astype(jnp.bfloat16)


def product(left, right):
    return jnp.dot(left, right, preferred_element_type=jnp.float32)


def product_transposed(left, right):
    return lax.dot_general(
        left, right, (((1,), (1,)), ((), ())), preferred_element_type=jnp.float32
    )


def whiten_kernel(
    lag_ref, wave_ref, bin_ref, high_ref, low_ref, halo_ref, band_ref, count_ref, out_ref, scratch
):
    rows = wave_ref.shape[0]
    segments = rows // PACK
    targets = out_ref.shape[0]
    wave = wave_ref[...]
    quarter = [wave[:, k * SPLIT : (k + 1) * SPLIT] for k in range(RADIX)]
    even_sum = quarter[0] + quarter[2]
    odd_sum = quarter[1] + quarter[3]
    even_high, even_low = split_float(quarter[0] - quarter[2])
    odd_high, odd_low = split_float(quarter[1] - quarter[3])
    real, imag = [None] * RADIX, [None] * RADIX
    for r, folded in ((0, even_sum + odd_sum), (2, even_sum - odd_sum)):
        folded_high, folded_low = split_float(folded)
        value = product(folded_high, high_ref[r]) + product(folded_low, high_ref[r])
        value = value + product(folded_high, low_ref[r])
        real[r] = value[:, :LANES]
        imag[r] = -value[:, LANES:]
    stacked_high = jnp.concatenate([even_high, odd_high], axis=0)
    stacked_low = jnp.concatenate([even_low, odd_low], axis=0)
    for r, sign in ((1, 1.0), (3, -1.0)):
        value = product(stacked_high, high_ref[r]) + product(stacked_low, high_ref[r])
        value = value + product(stacked_high, low_ref[r])
        real[r] = value[:rows, :LANES] - sign * value[rows:, LANES:]
        imag[r] = -value[:rows, LANES:] - sign * value[rows:, :LANES]
    beyond = product(wave.astype(jnp.bfloat16), halo_ref[...])
    parts = [jnp.sqrt(real[r] * real[r] + imag[r] * imag[r]) for r in range(RADIX)]
    side_real, side_imag = beyond[:, :LANES], beyond[:, LANES:]
    parts.append(jnp.sqrt(side_real * side_real + side_imag * side_imag))
    amplitude_high, amplitude_low = split_float(jnp.concatenate(parts, axis=1))
    total = product(amplitude_high, band_ref[...]) + product(amplitude_low, band_ref[...])
    inverse = 1.0 / (total * count_ref[...] + EPSILON)
    for r in range(RADIX):
        scale = inverse[:, r * LANES : (r + 1) * LANES]
        scratch[0, r] = real[r] * scale
        scratch[1, r] = imag[r] * scale
    width = LANES // targets
    chunk = lax.broadcasted_iota(jnp.int32, (PACK, LANES), 1) // width
    for pair in range(2):
        for part in range(2):
            rolled = []
            for half in range(2):
                for segment in range(segments):
                    rows_of = scratch[part, 2 * pair + half, pl.ds(segment, PACK, stride=segments), :]
                    shift = width * (half * segments + segment)
                    rolled.append(pltpu.roll(rows_of, shift, 1) if shift else rows_of)
            for target in range(targets):
                value = rolled[-target % targets]
                for place in range(1, targets):
                    value = jnp.where(chunk == place, rolled[(place - target) % targets], value)
                out_ref[target, 2 * pair + part] = value.astype(jnp.bfloat16)
    bins = bin_ref[...].astype(jnp.float32).astype(jnp.bfloat16)
    for target in range(targets):
        for k in range(bins.shape[1] // LANES):
            out_ref[target, 4 + k] = bins[:, k * LANES : (k + 1) * LANES]


def pair_kernel(group_ref, data_ref, out_ref, spectra, bins, cross, total):
    groups = data_ref.shape[0]
    stations = groups * PACK
    bin_count = total.shape[1]
    width = LANES // groups
    for group in range(groups):
        rows = pl.ds(group * PACK, PACK)
        for pair in range(2):
            for part in range(2):
                spectra[pair, rows, part * LANES : (part + 1) * LANES] = data_ref[
                    group, 2 * pair + part
                ]
        for k in range(stations // LANES):
            bins[rows, k * LANES : (k + 1) * LANES] = data_ref[group, 4 + k]
    total[...] = jnp.zeros_like(total)
    lane = lax.broadcasted_iota(jnp.int32, (PACK, 2 * LANES), 1) % LANES
    place = (lane // width - group_ref[0] + groups) % groups
    slot = place // (groups // 2) * width + lane % width
    row = lax.broadcasted_iota(jnp.int32, (PACK, 2 * LANES), 0)
    keep = (slot == row).astype(jnp.float32)[None]

    def one_group(group, first_column):
        start = pl.multiple_of(group * PACK, PACK)
        columns = stations - first_column
        for pair in range(2):
            own = spectra[pair, pl.ds(start, PACK), :].astype(jnp.float32)
            turned = jnp.concatenate([-own[:, LANES:], own[:, :LANES]], axis=1)
            diagonal = jnp.concatenate(
                [own[:, None, :] * keep, turned[:, None, :] * keep], axis=1
            ).astype(jnp.bfloat16)
            value = product_transposed(
                diagonal.reshape(PACK * 2 * PACK, 2 * LANES), spectra[pair, first_column:, :]
            )
            cross[:, pair * 2 * PACK : (pair + 1) * 2 * PACK, first_column:] = value.astype(
                jnp.bfloat16
            ).reshape(PACK, 2 * PACK, columns)
        column = first_column + lax.broadcasted_iota(jnp.int32, (PACK, columns), 1)
        station = start + lax.broadcasted_iota(jnp.int32, (PACK, columns), 0)
        own_bins = bins[pl.ds(start, PACK), first_column:].astype(jnp.float32)
        own_bins = jnp.where(column > station, own_bins, -1.0)
        wanted = lax.broadcasted_iota(jnp.int32, (bin_count, columns), 0).astype(jnp.float32)
        value = total[...]
        for i in range(PACK):
            onehot = (own_bins[i : i + 1, :] == wanted).astype(jnp.float32).astype(jnp.bfloat16)
            value = value + product_transposed(cross[i, :, first_column:], onehot)
        total[...] = value

    for block in range(stations // LANES):
        per_block = LANES // PACK

        def body(group, carry, first_column=block * LANES):
            one_group(group, first_column)
            return carry

        lax.fori_loop(block * per_block, (block + 1) * per_block, body, 0)
    out_ref[...] = total[...].T


def lag_kernel(lag_ref, data_ref, high_ref, low_ref, own_ref, swapped_ref, out_ref):
    sources, owned, width = data_ref.shape
    lane = lax.broadcasted_iota(jnp.int32, (owned, LANES), 1)
    is_real = lane % (2 * PACK) < PACK
    per_tile = LANES // width
    blocks = out_ref.shape[1] // LANES
    turned = [[] for _ in range(blocks)]
    for tile in range(sources // per_tile):
        value = jnp.concatenate(
            [data_ref[tile * per_tile + k] for k in range(per_tile)], axis=1
        )
        partner = jnp.where(
            is_real, pltpu.roll(value, LANES - PACK, 1), pltpu.roll(value, PACK, 1)
        )
        at = slice(tile * LANES, (tile + 1) * LANES)
        for block in range(blocks):
            turned[block].append(
                value * own_ref[block : block + 1, at] + partner * swapped_ref[block : block + 1, at]
            )
    left = jnp.concatenate([jnp.concatenate(row, axis=1) for row in turned], axis=0)
    left_high, left_low = split_float(left)
    value = product(left_high, high_ref[...]) + product(left_low, high_ref[...])
    value = value + product(left_high, low_ref[...])
    for block in range(blocks):
        out_ref[:, block * LANES : (block + 1) * LANES] = value[block * owned : (block + 1) * owned]


def whole_block(array):
    return pl.BlockSpec(array.shape, lambda i, s: (0,) * array.ndim)


def lag_part(array):
    return pl.BlockSpec(
        (None,) + array.shape[1:], lambda i, s: (s[0],) + (0,) * (array.ndim - 1)
    )


def call(kernel, scalar, arrays, specs, out_shape, scratch=()):
    grid_spec = pltpu.PrefetchScalarGridSpec(
        num_scalar_prefetch=1,
        grid=(1,),
        in_specs=specs,
        out_specs=whole_block(out_shape),
        scratch_shapes=list(scratch),
    )
    return pl.pallas_call(
        kernel,
        grid_spec=grid_spec,
        out_shape=out_shape,
        compiler_params=pltpu.CompilerParams(vmem_limit_bytes=48 << 20),
    )(scalar, *arrays)


def local_by_frequency(waveforms, pair_bin):
    station_count, segments, _ = waveforms.shape
    groups = lax.axis_size("grp")
    lag_count = lax.axis_size("lag")
    freq_count = NFFT // 2 // lag_count
    stations = station_count * groups
    bin_count = BIN_DEV * groups
    lag_index = lax.axis_index("lag").astype(jnp.int32).reshape(1)
    group_index = lax.axis_index("grp").astype(jnp.int32).reshape(1)
    rows = waveforms.reshape(station_count * segments, NFFT)
    tables = [jnp.asarray(t) for t in forward_constants(freq_count, lag_count)]
    blocks = 4 + stations // LANES
    whitened = call(
        whiten_kernel,
        lag_index,
        [rows, pair_bin, *tables],
        [whole_block(rows), whole_block(pair_bin), *[lag_part(t) for t in tables]],
        jax.ShapeDtypeStruct((groups, blocks, PACK, LANES), jnp.bfloat16),
        [pltpu.VMEM((2, RADIX, station_count * segments, LANES), jnp.float32)],
    )
    received = lax.all_to_all(whitened, "grp", 0, 0, tiled=True)
    binned = call(
        pair_kernel,
        group_index,
        [received],
        [whole_block(received)],
        jax.ShapeDtypeStruct((bin_count, 4 * PACK), jnp.float32),
        [
            pltpu.VMEM((2, stations, 2 * LANES), jnp.bfloat16),
            pltpu.VMEM((stations, stations), jnp.bfloat16),
            pltpu.VMEM((PACK, 4 * PACK, stations), jnp.bfloat16),
            pltpu.VMEM((4 * PACK, bin_count), jnp.float32),
        ],
    )
    outgoing = jnp.broadcast_to(
        binned.reshape(groups, 1, BIN_DEV, 4 * PACK), (groups, lag_count, BIN_DEV, 4 * PACK)
    ).reshape(groups * lag_count, BIN_DEV, 4 * PACK)
    owned = lax.all_to_all(outgoing, ("grp", "lag"), 0, 0, tiled=True)
    high, low, own, swapped = [
        jnp.asarray(t) for t in inverse_constants(freq_count, lag_count, groups)
    ]
    return call(
        lag_kernel,
        lag_index,
        [owned, high, low, own, swapped],
        [whole_block(owned), whole_block(high), whole_block(low), lag_part(own), lag_part(swapped)],
        jax.ShapeDtypeStruct((BIN_DEV, LAGS // lag_count), jnp.float32),
    )


def fits_by_frequency(mesh, waveforms):
    groups, lag_count = mesh.shape["grp"], mesh.shape["lag"]
    stations, segments, _ = waveforms.shape
    freq_count = NFFT // 2 // lag_count
    return (
        lag_count == 2
        and stations == groups * PACK
        and freq_count == RADIX * LANES
        and segments * 2 * (LANES // groups) == LANES
        and groups * BIN_DEV <= 256
    )


def solution(mesh):
    in_specs = (P("grp", None, None), P("grp", None))
    out_specs = P("grp", "lag")

    def run(waveforms, pair_bin):
        body = local_by_frequency if fits_by_frequency(mesh, waveforms) else local
        return jax.shard_map(
            body, mesh=mesh, in_specs=in_specs, out_specs=out_specs, check_vma=False
        )(waveforms, pair_bin)

    return run
```

```python
import math

import jax
import jax.numpy as jnp
import ml_dtypes
import numpy as np
from jax import lax
from jax.experimental import pallas as pl
from jax.experimental.pallas import tpu as pltpu
from jax.sharding import PartitionSpec as P

NFFT = 2048
LAGS = 1024
HW = 32
BIN_DEV = 8


EPSILON = 1e-06


def with_halo(block, sides, width):
    for axis, dim in sides:
        count = lax.axis_size(axis)
        forward = [(i, i + 1) for i in range(count - 1)]
        backward = [(target, source) for source, target in forward]
        low = lax.ppermute(
            lax.slice_in_dim(block, block.shape[dim] - width, None, axis=dim), axis, forward
        )
        high = lax.ppermute(lax.slice_in_dim(block, 0, width, axis=dim), axis, backward)
        block = jnp.concatenate([low, block, high], axis=dim)
    return block


def forward_table(freq_start, freq_count):
    sample_index = jnp.arange(NFFT, dtype=jnp.int32)[:, None]
    bin_index = freq_start + jnp.arange(freq_count, dtype=jnp.int32)[None, :]
    phase = (sample_index * bin_index % NFFT).astype(jnp.float32) * (2.0 * math.pi / NFFT)
    return jnp.concatenate([jnp.cos(phase), -jnp.sin(phase)], axis=1)


def inverse_table(freq_start, freq_count):
    bin_index = freq_start + jnp.arange(freq_count, dtype=jnp.int32)
    shifted = jnp.arange(LAGS, dtype=jnp.int32) - LAGS // 2
    phase = (bin_index[:, None] * shifted[None, :] % NFFT).astype(jnp.float32) * (
        2.0 * math.pi / NFFT
    )
    weight = jnp.where(bin_index == 0, 1.0, 2.0).astype(jnp.float32)[:, None] / NFFT
    return jnp.concatenate([weight * jnp.cos(phase), -weight * jnp.sin(phase)], axis=0)


def window_band(freq_count):
    padded_index = jnp.arange(freq_count + 2 * HW, dtype=jnp.int32)[:, None]
    bin_index = jnp.arange(freq_count, dtype=jnp.int32)[None, :]
    inside = (padded_index >= bin_index) & (padded_index <= bin_index + 2 * HW)
    return inside.astype(jnp.float32)


def window_count(freq_start, freq_count, half_length):
    bin_index = freq_start + jnp.arange(freq_count, dtype=jnp.int32)
    upper = jnp.minimum(bin_index + HW, half_length - 1)
    lower = jnp.maximum(bin_index - HW, 0)
    return (upper - lower + 1).astype(jnp.float32)


def add_block(running, whitened, remote, column_start, keep_pairs, imag_sign, pair_bin):
    freq_count = whitened.shape[2] // 2
    row_count = whitened.shape[0]
    column_count = remote.shape[0]
    own_real = whitened[..., :freq_count]
    own_imag = whitened[..., freq_count:]
    far_real = remote[..., :freq_count]
    far_imag = remote[..., freq_count:]
    own_stack = jnp.concatenate([own_real, own_imag], axis=1)
    own_alt = jnp.concatenate([own_real, -own_imag], axis=1)
    far_stack = jnp.concatenate([far_real, far_imag], axis=1)
    far_alt = jnp.concatenate([far_imag, far_real], axis=1)
    real_sum = jnp.einsum("asf,bsf->abf", own_stack, far_stack, preferred_element_type=jnp.float32)
    imag_sum = (
        jnp.einsum("asf,bsf->abf", own_alt, far_alt, preferred_element_type=jnp.float32) * imag_sign
    )
    cross = jnp.concatenate([real_sum, imag_sum], axis=2).astype(jnp.bfloat16)
    cross = cross.reshape(row_count * column_count, 2 * freq_count)
    block_bins = lax.dynamic_slice_in_dim(pair_bin, column_start, column_count, 1)
    block_bins = jnp.where(keep_pairs, block_bins, -1).reshape(-1)
    onehot = (block_bins[None, :] == jnp.arange(running.shape[0], dtype=jnp.int32)[:, None]).astype(
        jnp.bfloat16
    )
    return running + jnp.dot(onehot, cross, preferred_element_type=jnp.float32)


def local(waveforms, pair_bin):
    station_count = waveforms.shape[0]
    segments = waveforms.shape[1]
    groups = lax.axis_size("grp")
    group_index = lax.axis_index("grp")
    half_length = NFFT // 2
    freq_count = half_length // lax.axis_size("lag")
    freq_start = lax.axis_index("lag") * freq_count
    spectra = jnp.dot(
        waveforms.reshape(station_count * segments, NFFT),
        forward_table(freq_start, freq_count),
        precision=lax.Precision.HIGHEST,
        preferred_element_type=jnp.float32,
    )
    spectra = spectra.reshape(station_count, segments, 2 * freq_count)
    real_part = spectra[..., :freq_count]
    imag_part = spectra[..., freq_count:]
    amplitude = jnp.sqrt(real_part * real_part + imag_part * imag_part)
    padded = with_halo(amplitude, (("lag", 2),), HW)
    smoothed = jnp.dot(
        padded.reshape(station_count * segments, freq_count + 2 * HW),
        window_band(freq_count),
        precision=lax.Precision.HIGHEST,
        preferred_element_type=jnp.float32,
    )
    smoothed = smoothed.reshape(station_count, segments, freq_count) / window_count(
        freq_start, freq_count, half_length
    )
    whitened = jnp.concatenate(
        [real_part / (smoothed + EPSILON), imag_part / (smoothed + EPSILON)], axis=2
    ).astype(jnp.bfloat16)
    bins_total = BIN_DEV * groups
    row_start = group_index * station_count
    initial = jnp.zeros((bins_total, 2 * freq_count), jnp.float32)
    local_rows = jnp.arange(station_count, dtype=jnp.int32)
    remote = lax.all_gather(whitened, "grp", axis=0, tiled=True)
    group_total = remote.shape[0] // station_count
    per_step = max((divisor for divisor in (4, 3, 2, 1) if group_total % divisor == 0))
    step_count = group_total // per_step
    block_width = per_step * station_count
    blocks = remote.reshape(step_count, block_width, remote.shape[1], remote.shape[2])

    def one_step(step_index, carried):
        column_block = lax.dynamic_index_in_dim(blocks, step_index, 0, keepdims=False)
        column_start = step_index * block_width
        column_index = column_start + jnp.arange(block_width, dtype=jnp.int32)
        keep_pairs = column_index[None, :] > (row_start + local_rows)[:, None]

        def compute(accumulated):
            return add_block(
                accumulated, whitened, column_block, column_start, keep_pairs, 1.0, pair_bin
            )

        return lax.cond(
            column_start + block_width > row_start,
            compute,
            lambda accumulated: accumulated,
            carried,
        )

    binned = lax.fori_loop(0, step_count, one_step, initial)
    inverse = inverse_table(freq_start, freq_count)
    owned_bins = lax.psum_scatter(binned, "grp", scatter_dimension=0, tiled=True)
    lag_partial = jnp.dot(
        owned_bins, inverse, precision=lax.Precision.HIGHEST, preferred_element_type=jnp.float32
    )
    return lax.psum_scatter(lag_partial, "lag", scatter_dimension=1, tiled=True)


LANES = 128
RADIX = 4
SPLIT = NFFT // RADIX
PACK = 16


def halves(table):
    wide = np.asarray(table, np.float32)
    high = wide.astype(ml_dtypes.bfloat16)
    return high, (wide - high.astype(np.float32)).astype(ml_dtypes.bfloat16)


def forward_constants(freq_count, lag_count):
    steps = freq_count // RADIX
    sample = np.arange(SPLIT)
    width = HW // RADIX
    beyond = np.stack([steps + np.arange(width), np.arange(width) - width])
    beyond = beyond.reshape(-1)
    table = np.zeros((SPLIT, 4 * LANES))
    angle = 2.0 * np.pi / SPLIT * (sample[:, None] * np.arange(steps)[None, :] % SPLIT)
    table[:, :steps] = np.cos(angle)
    table[:, LANES : LANES + steps] = np.sin(angle)
    angle = 2.0 * np.pi / SPLIT * (sample[:, None] * beyond[None, :] % SPLIT)
    table[:, 2 * LANES : 2 * LANES + beyond.size] = np.cos(angle)
    table[:, 3 * LANES : 3 * LANES + beyond.size] = np.sin(angle)
    high, low = halves(table)
    tables = np.concatenate([high, low[:, : 2 * LANES]], axis=1)
    order = np.concatenate([np.arange(steps) * RADIX + r for r in range(RADIX)])
    outside = np.concatenate([beyond * RADIX + r for r in range(RADIX)])
    seen = np.concatenate([order, outside])
    band = np.zeros((freq_count + LANES, freq_count))
    band[: seen.size] = np.abs(seen[:, None] - order[None, :]) <= HW
    small = np.zeros((lag_count, 2 * RADIX + 8, freq_count), np.float32)
    for index in range(lag_count):
        start = index * freq_count
        for r in range(RADIX):
            angle = 2.0 * np.pi / NFFT * ((start + r) * sample % NFFT)
            small[index, 2 * r] = np.cos(angle)
            small[index, 2 * r + 1] = np.sin(angle)
        upper = np.minimum(start + order + HW, NFFT // 2 - 1)
        lower = np.maximum(start + order - HW, 0)
        small[index, 2 * RADIX] = 1.0 / (upper - lower + 1)
        there = (start + outside >= 0) & (start + outside < NFFT // 2)
        small[index, 2 * RADIX + 1, : outside.size] = there
    return small, tables, band.astype(ml_dtypes.bfloat16)


def inverse_constants(freq_count, lag_count, groups):
    run = freq_count // groups
    quarter = run // RADIX
    index = np.arange(groups * lag_count)
    start = (index % lag_count) * freq_count + (index // lag_count) * run
    pair, half, step = np.meshgrid(np.arange(2), np.arange(2), np.arange(quarter), indexing="ij")
    offset = (RADIX * step + 2 * pair + half).reshape(2, PACK)
    bins = start[:, None, None] + offset[None]
    both = np.stack([bins, bins], axis=2)
    imaginary = np.stack([np.zeros_like(bins), np.ones_like(bins)], axis=2).reshape(-1)
    both = both.reshape(-1)
    angle = 2.0 * np.pi / NFFT * (both[:, None] * np.arange(LANES)[None, :] % NFFT)
    table = np.where(imaginary[:, None] == 1, -np.sin(angle), np.cos(angle))
    table_high, table_low = halves(table)
    lag_block = LAGS // lag_count
    weight = np.where(both == 0, 1.0, 2.0) / NFFT
    own, swapped = [], []
    for lag in range(lag_count):
        first = np.arange(lag_block // LANES) * LANES + lag * lag_block - LAGS // 2
        angle = 2.0 * np.pi / NFFT * (both[None, :] * first[:, None] % NFFT)
        own.append(weight * np.cos(angle))
        swapped.append(np.where(imaginary == 1, 1.0, -1.0) * weight * np.sin(angle))
    return (
        table_high,
        table_low,
        np.stack(own).astype(np.float32),
        np.stack(swapped).astype(np.float32),
    )


def split_float(value):
    high = value.astype(jnp.bfloat16)
    return high, (value - high.astype(jnp.float32)).astype(jnp.bfloat16)


def product(left, right):
    return jnp.dot(left, right, preferred_element_type=jnp.float32)


def product_transposed(left, right):
    return lax.dot_general(
        left, right, (((1,), (1,)), ((), ())), preferred_element_type=jnp.float32
    )


def whiten_kernel(
    place_ref, bin_ref, wave_hbm, small_hbm, table_hbm, band_hbm, out_ref,
    wave_ref, small_ref, table_ref, band_ref, scratch, sems,
):
    rows = wave_ref.shape[0]
    segments = rows // PACK
    targets = out_ref.shape[0]
    copies = [
        pltpu.make_async_copy(source, target, sems.at[k])
        for k, (source, target) in enumerate(
            (
                (small_hbm.at[place_ref[1]], small_ref),
                (wave_hbm, wave_ref),
                (table_hbm, table_ref),
                (band_hbm, band_ref),
            )
        )
    ]
    for copy in copies:
        copy.start()
    stations = bin_ref.shape[1]
    turned = pltpu.roll(
        bin_ref[...].astype(jnp.float32), (stations - place_ref[0] * PACK) % stations, 1
    )
    following = jnp.concatenate(
        [
            pltpu.roll(turned[i : i + 1, :], stations - 1 - i, 1)[:, : stations // 2]
            for i in range(PACK)
        ],
        axis=0,
    ).astype(jnp.bfloat16)
    for target in range(targets):
        out_ref[target, 4] = following
    copies[0].wait()
    copies[1].wait()
    quarter = [wave_ref[:, k * SPLIT : (k + 1) * SPLIT] for k in range(RADIX)]
    even_sum, odd_sum = quarter[0] + quarter[2], quarter[1] + quarter[3]
    even, odd = quarter[0] - quarter[2], quarter[1] - quarter[3]
    high, low = [], []
    for r, first, second in (
        (0, even_sum + odd_sum, None), (1, even, -odd), (2, even_sum - odd_sum, None), (3, even, odd)
    ):
        cosine, sine = small_ref[2 * r : 2 * r + 1, :], small_ref[2 * r + 1 : 2 * r + 2, :]
        turned_real, turned_imag = first * cosine, -first * sine
        if second is not None:
            turned_real = turned_real + second * sine
            turned_imag = turned_imag + second * cosine
        for value in (turned_real, turned_imag):
            value_high, value_low = split_float(value)
            high.append(value_high)
            low.append(value_low)
    high = jnp.concatenate(high, axis=0)
    low = jnp.concatenate(low, axis=0)
    copies[2].wait()
    main, side, rest = (slice(k * 2 * LANES, (k + 1) * 2 * LANES) for k in range(3))
    value = product(high, table_ref[:, main]) + product(low, table_ref[:, main])
    value = value + product(high, table_ref[:, rest])
    beyond = product(high, table_ref[:, side])

    def parts_of(pair, r):
        first = pair[2 * r * rows : (2 * r + 1) * rows]
        second = pair[(2 * r + 1) * rows : (2 * r + 2) * rows]
        return first[:, :LANES] + second[:, LANES:], second[:, :LANES] - first[:, LANES:]

    spectra = [parts_of(value, r) for r in range(RADIX)]
    amplitudes = [jnp.sqrt(real * real + imag * imag) for real, imag in spectra]
    width = 2 * HW // RADIX
    outside = None
    for r in range(RADIX):
        real, imag = parts_of(beyond, r)
        amplitude = jnp.sqrt(real * real + imag * imag)
        outside = outside + pltpu.roll(amplitude, r * width, 1) if r else amplitude
    amplitudes.append(outside * small_ref[2 * RADIX + 1 : 2 * RADIX + 2, :LANES])
    amplitude_high, amplitude_low = split_float(jnp.concatenate(amplitudes, axis=1))
    copies[3].wait()
    total = product(amplitude_high, band_ref[...]) + product(amplitude_low, band_ref[...])
    inverse = 1.0 / (total * small_ref[2 * RADIX : 2 * RADIX + 1, :] + EPSILON)
    for r, (real, imag) in enumerate(spectra):
        scale = inverse[:, r * LANES : (r + 1) * LANES]
        scratch[0, r] = real * scale
        scratch[1, r] = imag * scale
    width = LANES // targets
    chunk = lax.broadcasted_iota(jnp.int32, (PACK, LANES), 1) // width
    for pair in range(2):
        for part in range(2):
            rolled = []
            for half in range(2):
                for segment in range(segments):
                    rows_of = scratch[part, 2 * pair + half, pl.ds(segment, PACK, stride=segments), :]
                    shift = width * (half * segments + segment)
                    rolled.append(pltpu.roll(rows_of, shift, 1) if shift else rows_of)
            for target in range(targets):
                value = rolled[-target % targets]
                for place in range(1, targets):
                    value = jnp.where(chunk == place, rolled[(place - target) % targets], value)
                out_ref[target, 2 * pair + part] = value.astype(jnp.bfloat16)


def pair_kernel(place_ref, data_ref, out_ref, spectra, cross, total):
    groups = data_ref.shape[0]
    stations = groups * PACK
    bin_count = total.shape[0]
    width = LANES // groups
    half = stations // 2
    for group in range(groups):
        for pair in range(2):
            for part in range(2):
                spectra[
                    pair, group * PACK : (group + 1) * PACK, part * LANES : (part + 1) * LANES
                ] = data_ref[group, 2 * pair + part]
    total[...] = jnp.zeros_like(total)
    lane = lax.broadcasted_iota(jnp.int32, (PACK, 2 * LANES), 1) % LANES
    place = (lane // width - place_ref[0] + groups) % groups
    slot = place // (groups // 2) * width + lane % width
    row = lax.broadcasted_iota(jnp.int32, (PACK, 2 * LANES), 0)
    keep = (slot == row).astype(jnp.float32)
    keep_own = keep.astype(jnp.bfloat16)
    keep_turned = jnp.concatenate([-keep[:, :LANES], keep[:, LANES:]], axis=1).astype(jnp.bfloat16)
    wanted = lax.broadcasted_iota(jnp.int32, (bin_count, stations), 0).astype(jnp.float32)
    wanted = wanted.astype(jnp.bfloat16)
    one, zero = jnp.bfloat16(1), jnp.bfloat16(0)

    def spread(value):
        return jnp.broadcast_to(value, (PACK, value.shape[1])).astype(jnp.bfloat16)

    def diagonal(pair, start):
        own = spectra[pair, start : start + PACK, :].astype(jnp.float32)
        parts = []
        for i in range(PACK):
            value = spread(own[i : i + 1, :])
            swapped = jnp.concatenate([value[:, LANES:], value[:, :LANES]], axis=1)
            parts += [value * keep_own, swapped * keep_turned]
        return jnp.concatenate(parts, axis=0)

    station = lax.broadcasted_iota(jnp.int32, (PACK, stations), 0)
    column = lax.broadcasted_iota(jnp.int32, (PACK, stations), 1)
    for number in range(groups // 2):
        buffer = number % cross.shape[0]
        low = number * PACK
        own = low + station
        near = (column > own) & (column <= own + half)
        sign = jnp.where(column < own, -1.0, 1.0)
        for pair in range(2):
            left = jnp.concatenate([diagonal(pair, low), diagonal(pair, low + half)], axis=0)
            value = product_transposed(left, spectra[pair])
            rows = slice(pair * 2 * PACK, (pair + 1) * 2 * PACK)
            for i in range(PACK):
                first = value[i * 2 * PACK : (i + 1) * 2 * PACK]
                second = value[(PACK + i) * 2 * PACK : (PACK + i + 1) * 2 * PACK]
                second = jnp.concatenate([second[:PACK], second[PACK:] * sign[i : i + 1]], axis=0)
                merged = jnp.where(near[i : i + 1], first, second).astype(jnp.bfloat16)
                cross[buffer, rows, i * stations : (i + 1) * stations] = merged
        following = jnp.concatenate(
            [data_ref[number, 4], data_ref[number + groups // 2, 4]], axis=1
        ).astype(jnp.float32)
        shared = pltpu.roll(following, low + 1, 1, stride=1, stride_axis=0)
        shared = jnp.where(column == own, -1.0, shared)
        hot = []
        for i in range(PACK):
            value = spread(shared[i : i + 1, :])
            hot.append(
                jnp.concatenate(
                    [
                        jnp.where(value == wanted[k : k + PACK], one, zero)
                        for k in range(0, bin_count, PACK)
                    ],
                    axis=0,
                )
            )
        total[...] += product_transposed(jnp.concatenate(hot, axis=1), cross[buffer])
    copies = out_ref.shape[0] // groups
    middle = BIN_DEV // 2
    for group in range(groups):
        upper = total[group * BIN_DEV : group * BIN_DEV + middle, :]
        lower = total[group * BIN_DEV + middle : (group + 1) * BIN_DEV, :]
        value = jnp.concatenate([upper, lower], axis=1)
        for k in range(copies):
            out_ref[group * copies + k] = value


def lag_kernel(place_ref, data_ref, high_ref, low_ref, own_ref, swapped_ref, out_ref):
    sources = data_ref.shape[0]
    owned, blocks = out_ref.shape[0], out_ref.shape[1] // LANES
    lane = lax.broadcasted_iota(jnp.int32, (owned, LANES), 1)
    is_real = lane % (2 * PACK) < PACK
    is_first = lane[: owned // 2] < LANES // 2
    turned = [[] for _ in range(blocks)]
    for tile in range(sources // 2):
        first, second = data_ref[2 * tile], data_ref[2 * tile + 1]
        value = jnp.concatenate(
            [
                jnp.where(is_first, first, pltpu.roll(second, LANES // 2, 1)),
                jnp.where(is_first, pltpu.roll(first, LANES // 2, 1), second),
            ],
            axis=0,
        )
        partner = jnp.where(
            is_real, pltpu.roll(value, LANES - PACK, 1), pltpu.roll(value, PACK, 1)
        )
        at = slice(tile * LANES, (tile + 1) * LANES)
        for block in range(blocks):
            turned[block].append(
                value * own_ref[block : block + 1, at] + partner * swapped_ref[block : block + 1, at]
            )
    left = jnp.concatenate([jnp.concatenate(row, axis=1) for row in turned], axis=0)
    left_high, left_low = split_float(left)
    value = product(left_high, high_ref[...]) + product(left_low, high_ref[...])
    value = value + product(left_high, low_ref[...])
    for block in range(blocks):
        out_ref[:, block * LANES : (block + 1) * LANES] = value[block * owned : (block + 1) * owned]


def whole_block(array):
    return pl.BlockSpec(array.shape, lambda i, s: (0,) * array.ndim)


def lag_part(array):
    return pl.BlockSpec(
        (None,) + array.shape[1:], lambda i, s: (s[1],) + (0,) * (array.ndim - 1)
    )


def call(kernel, scalar, arrays, specs, out_shape, scratch=()):
    grid_spec = pltpu.PrefetchScalarGridSpec(
        num_scalar_prefetch=1,
        grid=(1,),
        in_specs=specs,
        out_specs=whole_block(out_shape),
        scratch_shapes=list(scratch),
    )
    return pl.pallas_call(
        kernel,
        grid_spec=grid_spec,
        out_shape=out_shape,
        compiler_params=pltpu.CompilerParams(vmem_limit_bytes=48 << 20),
    )(scalar, *arrays)


def local_by_frequency(waveforms, pair_bin):
    station_count, segments, _ = waveforms.shape
    groups = lax.axis_size("grp")
    lag_count = lax.axis_size("lag")
    freq_count = NFFT // 2 // lag_count
    stations = station_count * groups
    bin_count = BIN_DEV * groups
    place = jnp.stack([lax.axis_index("grp"), lax.axis_index("lag")]).astype(jnp.int32)
    rows = waveforms.reshape(station_count * segments, NFFT)
    small, tables, band = [jnp.asarray(t) for t in forward_constants(freq_count, lag_count)]
    far = [pltpu.with_memory_space_constraint(v, pltpu.HBM) for v in (rows, small, tables, band)]
    whitened = call(
        whiten_kernel,
        place,
        [pair_bin, *far],
        [whole_block(pair_bin)] + [pl.BlockSpec(memory_space=pltpu.HBM)] * 4,
        jax.ShapeDtypeStruct((groups, 5, PACK, LANES), jnp.bfloat16),
        [
            pltpu.VMEM(rows.shape, jnp.float32),
            pltpu.VMEM(small.shape[1:], jnp.float32),
            pltpu.VMEM(tables.shape, jnp.bfloat16),
            pltpu.VMEM(band.shape, jnp.bfloat16),
            pltpu.VMEM((2, RADIX, station_count * segments, LANES), jnp.float32),
            pltpu.SemaphoreType.DMA((4,)),
        ],
    )
    received = lax.all_to_all(whitened, "grp", 0, 0, tiled=True)
    outgoing = call(
        pair_kernel,
        place,
        [received],
        [whole_block(received)],
        jax.ShapeDtypeStruct((groups * lag_count, BIN_DEV // 2, LANES), jnp.float32),
        [
            pltpu.VMEM((2, stations, 2 * LANES), jnp.bfloat16),
            pltpu.VMEM((2, 4 * PACK, PACK * stations), jnp.bfloat16),
            pltpu.VMEM((bin_count, 4 * PACK), jnp.float32),
        ],
    )
    owned = lax.all_to_all(outgoing, ("grp", "lag"), 0, 0, tiled=True)
    high, low, own, swapped = [
        jnp.asarray(t) for t in inverse_constants(freq_count, lag_count, groups)
    ]
    return call(
        lag_kernel,
        place,
        [owned, high, low, own, swapped],
        [whole_block(owned), whole_block(high), whole_block(low), lag_part(own), lag_part(swapped)],
        jax.ShapeDtypeStruct((BIN_DEV, LAGS // lag_count), jnp.float32),
    )


def fits_by_frequency(mesh, waveforms):
    groups, lag_count = mesh.shape["grp"], mesh.shape["lag"]
    stations, segments, _ = waveforms.shape
    freq_count = NFFT // 2 // lag_count
    return (
        lag_count == 2
        and stations == groups * PACK == 2 * LANES
        and freq_count == RADIX * LANES
        and segments * 2 * (LANES // groups) == LANES
        and groups * BIN_DEV <= 256
    )


def solution(mesh):
    in_specs = (P("grp", None, None), P("grp", None))
    out_specs = P("grp", "lag")

    def run(waveforms, pair_bin):
        body = local_by_frequency if fits_by_frequency(mesh, waveforms) else local
        return jax.shard_map(
            body, mesh=mesh, in_specs=in_specs, out_specs=out_specs, check_vma=False
        )(waveforms, pair_bin)

    return run
```

```python
import math

import jax
import jax.numpy as jnp
import ml_dtypes
import numpy as np
from jax import lax
from jax.experimental import pallas as pl
from jax.experimental.pallas import tpu as pltpu
from jax.sharding import PartitionSpec as P

NFFT = 2048
LAGS = 1024
HW = 32
BIN_DEV = 8


EPSILON = 1e-06


def with_halo(block, sides, width):
    for axis, dim in sides:
        count = lax.axis_size(axis)
        forward = [(i, i + 1) for i in range(count - 1)]
        backward = [(target, source) for source, target in forward]
        low = lax.ppermute(
            lax.slice_in_dim(block, block.shape[dim] - width, None, axis=dim), axis, forward
        )
        high = lax.ppermute(lax.slice_in_dim(block, 0, width, axis=dim), axis, backward)
        block = jnp.concatenate([low, block, high], axis=dim)
    return block


def forward_table(freq_start, freq_count):
    sample_index = jnp.arange(NFFT, dtype=jnp.int32)[:, None]
    bin_index = freq_start + jnp.arange(freq_count, dtype=jnp.int32)[None, :]
    phase = (sample_index * bin_index % NFFT).astype(jnp.float32) * (2.0 * math.pi / NFFT)
    return jnp.concatenate([jnp.cos(phase), -jnp.sin(phase)], axis=1)


def inverse_table(freq_start, freq_count):
    bin_index = freq_start + jnp.arange(freq_count, dtype=jnp.int32)
    shifted = jnp.arange(LAGS, dtype=jnp.int32) - LAGS // 2
    phase = (bin_index[:, None] * shifted[None, :] % NFFT).astype(jnp.float32) * (
        2.0 * math.pi / NFFT
    )
    weight = jnp.where(bin_index == 0, 1.0, 2.0).astype(jnp.float32)[:, None] / NFFT
    return jnp.concatenate([weight * jnp.cos(phase), -weight * jnp.sin(phase)], axis=0)


def window_band(freq_count):
    padded_index = jnp.arange(freq_count + 2 * HW, dtype=jnp.int32)[:, None]
    bin_index = jnp.arange(freq_count, dtype=jnp.int32)[None, :]
    inside = (padded_index >= bin_index) & (padded_index <= bin_index + 2 * HW)
    return inside.astype(jnp.float32)


def window_count(freq_start, freq_count, half_length):
    bin_index = freq_start + jnp.arange(freq_count, dtype=jnp.int32)
    upper = jnp.minimum(bin_index + HW, half_length - 1)
    lower = jnp.maximum(bin_index - HW, 0)
    return (upper - lower + 1).astype(jnp.float32)


def add_block(running, whitened, remote, column_start, keep_pairs, imag_sign, pair_bin):
    freq_count = whitened.shape[2] // 2
    row_count = whitened.shape[0]
    column_count = remote.shape[0]
    own_real = whitened[..., :freq_count]
    own_imag = whitened[..., freq_count:]
    far_real = remote[..., :freq_count]
    far_imag = remote[..., freq_count:]
    own_stack = jnp.concatenate([own_real, own_imag], axis=1)
    own_alt = jnp.concatenate([own_real, -own_imag], axis=1)
    far_stack = jnp.concatenate([far_real, far_imag], axis=1)
    far_alt = jnp.concatenate([far_imag, far_real], axis=1)
    real_sum = jnp.einsum("asf,bsf->abf", own_stack, far_stack, preferred_element_type=jnp.float32)
    imag_sum = (
        jnp.einsum("asf,bsf->abf", own_alt, far_alt, preferred_element_type=jnp.float32) * imag_sign
    )
    cross = jnp.concatenate([real_sum, imag_sum], axis=2).astype(jnp.bfloat16)
    cross = cross.reshape(row_count * column_count, 2 * freq_count)
    block_bins = lax.dynamic_slice_in_dim(pair_bin, column_start, column_count, 1)
    block_bins = jnp.where(keep_pairs, block_bins, -1).reshape(-1)
    onehot = (block_bins[None, :] == jnp.arange(running.shape[0], dtype=jnp.int32)[:, None]).astype(
        jnp.bfloat16
    )
    return running + jnp.dot(onehot, cross, preferred_element_type=jnp.float32)


def local(waveforms, pair_bin):
    station_count = waveforms.shape[0]
    segments = waveforms.shape[1]
    groups = lax.axis_size("grp")
    group_index = lax.axis_index("grp")
    half_length = NFFT // 2
    freq_count = half_length // lax.axis_size("lag")
    freq_start = lax.axis_index("lag") * freq_count
    spectra = jnp.dot(
        waveforms.reshape(station_count * segments, NFFT),
        forward_table(freq_start, freq_count),
        precision=lax.Precision.HIGHEST,
        preferred_element_type=jnp.float32,
    )
    spectra = spectra.reshape(station_count, segments, 2 * freq_count)
    real_part = spectra[..., :freq_count]
    imag_part = spectra[..., freq_count:]
    amplitude = jnp.sqrt(real_part * real_part + imag_part * imag_part)
    padded = with_halo(amplitude, (("lag", 2),), HW)
    smoothed = jnp.dot(
        padded.reshape(station_count * segments, freq_count + 2 * HW),
        window_band(freq_count),
        precision=lax.Precision.HIGHEST,
        preferred_element_type=jnp.float32,
    )
    smoothed = smoothed.reshape(station_count, segments, freq_count) / window_count(
        freq_start, freq_count, half_length
    )
    whitened = jnp.concatenate(
        [real_part / (smoothed + EPSILON), imag_part / (smoothed + EPSILON)], axis=2
    ).astype(jnp.bfloat16)
    bins_total = BIN_DEV * groups
    row_start = group_index * station_count
    initial = jnp.zeros((bins_total, 2 * freq_count), jnp.float32)
    local_rows = jnp.arange(station_count, dtype=jnp.int32)
    remote = lax.all_gather(whitened, "grp", axis=0, tiled=True)
    group_total = remote.shape[0] // station_count
    per_step = max((divisor for divisor in (4, 3, 2, 1) if group_total % divisor == 0))
    step_count = group_total // per_step
    block_width = per_step * station_count
    blocks = remote.reshape(step_count, block_width, remote.shape[1], remote.shape[2])

    def one_step(step_index, carried):
        column_block = lax.dynamic_index_in_dim(blocks, step_index, 0, keepdims=False)
        column_start = step_index * block_width
        column_index = column_start + jnp.arange(block_width, dtype=jnp.int32)
        keep_pairs = column_index[None, :] > (row_start + local_rows)[:, None]

        def compute(accumulated):
            return add_block(
                accumulated, whitened, column_block, column_start, keep_pairs, 1.0, pair_bin
            )

        return lax.cond(
            column_start + block_width > row_start,
            compute,
            lambda accumulated: accumulated,
            carried,
        )

    binned = lax.fori_loop(0, step_count, one_step, initial)
    inverse = inverse_table(freq_start, freq_count)
    owned_bins = lax.psum_scatter(binned, "grp", scatter_dimension=0, tiled=True)
    lag_partial = jnp.dot(
        owned_bins, inverse, precision=lax.Precision.HIGHEST, preferred_element_type=jnp.float32
    )
    return lax.psum_scatter(lag_partial, "lag", scatter_dimension=1, tiled=True)


LANES = 128
RADIX = 4
HALO = 2 * HW // RADIX
SPLIT = NFFT // RADIX
PACK = 16


def halves(table):
    wide = np.asarray(table, np.float32)
    high = wide.astype(ml_dtypes.bfloat16)
    return high, (wide - high.astype(np.float32)).astype(ml_dtypes.bfloat16)


def forward_constants(freq_count, lag_count):
    steps = freq_count // RADIX
    sample = np.arange(SPLIT)
    width = HW // RADIX
    beyond = np.stack([steps + np.arange(width), np.arange(width) - width])
    beyond = beyond.reshape(-1)
    table = np.zeros((SPLIT, 2 * LANES))
    side = np.zeros((SPLIT, LANES))
    angle = 2.0 * np.pi / SPLIT * (sample[:, None] * np.arange(steps)[None, :] % SPLIT)
    table[:, :steps] = np.cos(angle)
    table[:, LANES : LANES + steps] = np.sin(angle)
    angle = 2.0 * np.pi / SPLIT * (sample[:, None] * beyond[None, :] % SPLIT)
    side[:, : beyond.size] = np.cos(angle)
    side[:, LANES // 2 : LANES // 2 + beyond.size] = np.sin(angle)
    tables = np.concatenate([*halves(table), halves(side)[0]], axis=1)
    order = np.concatenate([np.arange(steps) * RADIX + r for r in range(RADIX)])
    outside = np.concatenate([beyond * RADIX + r for r in range(RADIX)])
    small = np.zeros((lag_count, 2 * RADIX + 8, freq_count), np.float32)
    for index in range(lag_count):
        start = index * freq_count
        for r in range(RADIX):
            angle = 2.0 * np.pi / NFFT * ((start + r) * sample % NFFT)
            small[index, 2 * r] = np.cos(angle)
            small[index, 2 * r + 1] = np.sin(angle)
        upper = np.minimum(start + order + HW, NFFT // 2 - 1)
        lower = np.maximum(start + order - HW, 0)
        small[index, 2 * RADIX] = 1.0 / (upper - lower + 1)
        there = (start + outside >= 0) & (start + outside < NFFT // 2)
        small[index, 2 * RADIX + 1, : outside.size] = there
    return small, tables


def inverse_constants(freq_count, lag_count, groups):
    run = freq_count // groups
    quarter = run // RADIX
    index = np.arange(groups * lag_count)
    start = (index % lag_count) * freq_count + (index // lag_count) * run
    pair, half, step = np.meshgrid(np.arange(2), np.arange(2), np.arange(quarter), indexing="ij")
    offset = (RADIX * step + 2 * pair + half).reshape(2, PACK)
    bins = start[:, None, None] + offset[None]
    both = np.stack([bins, bins], axis=2)
    imaginary = np.stack([np.zeros_like(bins), np.ones_like(bins)], axis=2).reshape(-1)
    both = both.reshape(-1)
    angle = 2.0 * np.pi / NFFT * (both[:, None] * np.arange(LANES)[None, :] % NFFT)
    table = np.where(imaginary[:, None] == 1, -np.sin(angle), np.cos(angle))
    table_high, table_low = halves(table)
    lag_block = LAGS // lag_count
    weight = np.where(both == 0, 1.0, 2.0) / NFFT
    own, swapped = [], []
    for lag in range(lag_count):
        first = np.arange(lag_block // LANES) * LANES + lag * lag_block - LAGS // 2
        angle = 2.0 * np.pi / NFFT * (both[None, :] * first[:, None] % NFFT)
        own.append(weight * np.cos(angle))
        swapped.append(np.where(imaginary == 1, 1.0, -1.0) * weight * np.sin(angle))
    return (
        table_high,
        table_low,
        np.stack(own).astype(np.float32),
        np.stack(swapped).astype(np.float32),
    )


def split_float(value):
    high = value.astype(jnp.bfloat16)
    return high, (value - high.astype(jnp.float32)).astype(jnp.bfloat16)


def product(left, right):
    return jnp.dot(left, right, preferred_element_type=jnp.float32)


def product_transposed(left, right):
    return lax.dot_general(
        left, right, (((1,), (1,)), ((), ())), preferred_element_type=jnp.float32
    )


def fill_band(band_ref):
    column = lax.broadcasted_iota(jnp.int32, (LANES, LANES), 1)
    row = lax.broadcasted_iota(jnp.int32, (LANES, LANES), 0)
    apart = RADIX * (row - column)
    near = {
        shift: (jnp.abs(apart + shift) <= HW).astype(jnp.float32).astype(jnp.bfloat16)
        for shift in range(1 - RADIX, RADIX)
    }
    place = row % HALO
    outer = row // HALO + RADIX * jnp.where(place < HALO // 2, LANES + place, place - HALO)
    for to in range(RADIX):
        at = slice(to * LANES, (to + 1) * LANES)
        for r in range(RADIX):
            band_ref[r * LANES : (r + 1) * LANES, at] = near[r - to]
        beside = (jnp.abs(outer - RADIX * column - to) <= HW) & (row < RADIX * HALO)
        band_ref[RADIX * LANES :, at] = beside.astype(jnp.float32).astype(jnp.bfloat16)


def whiten_kernel(
    bin_hbm, wave_hbm, small_hbm, table_hbm, out_ref,
    bin_ref, wave_ref, small_ref, table_ref, band_ref, scratch, sems,
):
    rows = wave_ref.shape[0]
    segments = rows // PACK
    targets = out_ref.shape[0]
    parts = 2
    part_rows = rows // parts
    moves = [(small_hbm.at[lax.axis_index("lag")], small_ref)]
    for k in range(parts):
        at = pl.ds(k * part_rows, part_rows)
        moves.append((wave_hbm.at[at], wave_ref.at[at]))
    moves += [(table_hbm, table_ref), (bin_hbm, bin_ref)]
    copies = [
        pltpu.make_async_copy(source, target, sems.at[k])
        for k, (source, target) in enumerate(moves)
    ]
    for copy in copies:
        copy.start()
    fill_band(band_ref)
    copies[0].wait()
    value, beyond = [], []
    main, rest = slice(0, 2 * LANES), slice(2 * LANES, 4 * LANES)
    side = slice(4 * LANES, 5 * LANES)
    for k in range(parts):
        copies[1 + k].wait()
        at = slice(k * part_rows, (k + 1) * part_rows)
        quarter = [wave_ref[at, j * SPLIT : (j + 1) * SPLIT] for j in range(RADIX)]
        even_sum, odd_sum = quarter[0] + quarter[2], quarter[1] + quarter[3]
        even, odd = quarter[0] - quarter[2], quarter[1] - quarter[3]
        high, low = [], []
        for r, first, second in (
            (0, even_sum + odd_sum, None), (1, even, -odd), (2, even_sum - odd_sum, None), (3, even, odd)
        ):
            cosine, sine = small_ref[2 * r : 2 * r + 1, :], small_ref[2 * r + 1 : 2 * r + 2, :]
            turned_real, turned_imag = first * cosine, -first * sine
            if second is not None:
                turned_real = turned_real + second * sine
                turned_imag = turned_imag + second * cosine
            for turned in (turned_real, turned_imag):
                turned_high, turned_low = split_float(turned)
                high.append(turned_high)
                low.append(turned_low)
        high = jnp.concatenate(high, axis=0)
        low = jnp.concatenate(low, axis=0)
        if k == 0:
            copies[1 + parts].wait()
        product_main = product(high, table_ref[:, main]) + product(low, table_ref[:, main])
        value.append(product_main + product(high, table_ref[:, rest]))
        beyond.append(product(high, table_ref[:, side]))
    copies[2 + parts].wait()
    stations = bin_ref.shape[1]
    turned = pltpu.roll(
        bin_ref[...].astype(jnp.float32), (stations - lax.axis_index("grp") * PACK) % stations, 1
    )
    following = jnp.concatenate(
        [
            pltpu.roll(turned[i : i + 1, :], stations - 1 - i, 1)[:, : stations // 2]
            for i in range(PACK)
        ],
        axis=0,
    ).astype(jnp.bfloat16)
    for target in range(targets):
        out_ref[target, 4] = following

    def both_of(pairs, r):
        first = [pair[2 * r * part_rows : (2 * r + 1) * part_rows] for pair in pairs]
        second = [pair[(2 * r + 1) * part_rows : (2 * r + 2) * part_rows] for pair in pairs]
        return jnp.concatenate(first, axis=0), jnp.concatenate(second, axis=0)

    def parts_of(r):
        first, second = both_of(value, r)
        return first[:, :LANES] + second[:, LANES:], second[:, :LANES] - first[:, LANES:]

    spectra = [parts_of(r) for r in range(RADIX)]
    amplitudes = [jnp.sqrt(real * real + imag * imag) for real, imag in spectra]
    outside = None
    for r in range(RADIX):
        first, second = both_of(beyond, r)
        real = first + pltpu.roll(second, LANES // 2, 1)
        imag = second - pltpu.roll(first, LANES // 2, 1)
        amplitude = jnp.sqrt(real * real + imag * imag)
        outside = outside + pltpu.roll(amplitude, r * HALO, 1) if r else amplitude
    amplitudes.append(outside * small_ref[2 * RADIX + 1 : 2 * RADIX + 2, :LANES])
    amplitude_high, amplitude_low = split_float(jnp.concatenate(amplitudes, axis=1))
    total = product(amplitude_high, band_ref[...]) + product(amplitude_low, band_ref[...])
    inverse = 1.0 / (total * small_ref[2 * RADIX : 2 * RADIX + 1, :] + EPSILON)
    for r, (real, imag) in enumerate(spectra):
        scale = inverse[:, r * LANES : (r + 1) * LANES]
        scratch[0, r] = real * scale
        scratch[1, r] = imag * scale
    width = LANES // targets
    chunk = lax.broadcasted_iota(jnp.int32, (PACK, LANES), 1) // width
    for pair in range(2):
        for part in range(2):
            rolled = []
            for half in range(2):
                for segment in range(segments):
                    rows_of = scratch[part, 2 * pair + half, pl.ds(segment, PACK, stride=segments), :]
                    shift = width * (half * segments + segment)
                    rolled.append(pltpu.roll(rows_of, shift, 1) if shift else rows_of)
            for target in range(targets):
                value = rolled[-target % targets]
                for place in range(1, targets):
                    value = jnp.where(chunk == place, rolled[(place - target) % targets], value)
                out_ref[target, 2 * pair + part] = value.astype(jnp.bfloat16)


def pair_kernel(data_ref, out_ref, spectra, cross, total):
    groups = data_ref.shape[0]
    stations = groups * PACK
    bin_count = total.shape[0]
    width = LANES // groups
    half = stations // 2
    for group in range(groups):
        for pair in range(2):
            for part in range(2):
                spectra[
                    pair, group * PACK : (group + 1) * PACK, part * LANES : (part + 1) * LANES
                ] = data_ref[group, 2 * pair + part]
    total[...] = jnp.zeros_like(total)
    lane = lax.broadcasted_iota(jnp.int32, (PACK, 2 * LANES), 1) % LANES
    place = (lane // width - lax.axis_index("grp") + groups) % groups
    slot = place // (groups // 2) * width + lane % width
    row = lax.broadcasted_iota(jnp.int32, (PACK, 2 * LANES), 0)
    keep = (slot == row).astype(jnp.float32)
    keep_own = keep.astype(jnp.bfloat16)
    keep_turned = jnp.concatenate([-keep[:, :LANES], keep[:, LANES:]], axis=1).astype(jnp.bfloat16)
    wanted = lax.broadcasted_iota(jnp.int32, (bin_count, stations), 0).astype(jnp.float32)
    wanted = wanted.astype(jnp.bfloat16)
    one, zero = jnp.bfloat16(1), jnp.bfloat16(0)

    def spread(value):
        return jnp.broadcast_to(value, (PACK, value.shape[1])).astype(jnp.bfloat16)

    def diagonal(pair, start):
        own = spectra[pair, start : start + PACK, :].astype(jnp.float32)
        parts = []
        for i in range(PACK):
            value = spread(own[i : i + 1, :])
            swapped = jnp.concatenate([value[:, LANES:], value[:, :LANES]], axis=1)
            parts += [value * keep_own, swapped * keep_turned]
        return jnp.concatenate(parts, axis=0)

    station = lax.broadcasted_iota(jnp.int32, (PACK, stations), 0)
    column = lax.broadcasted_iota(jnp.int32, (PACK, stations), 1)
    for number in range(groups // 2):
        buffer = number % cross.shape[0]
        low = number * PACK
        own = low + station
        near = (column > own) & (column <= own + half)
        sign = jnp.where(column < own, -1.0, 1.0)
        for pair in range(2):
            left = jnp.concatenate([diagonal(pair, low), diagonal(pair, low + half)], axis=0)
            value = product_transposed(left, spectra[pair])
            rows = slice(pair * 2 * PACK, (pair + 1) * 2 * PACK)
            for i in range(PACK):
                first = value[i * 2 * PACK : (i + 1) * 2 * PACK]
                second = value[(PACK + i) * 2 * PACK : (PACK + i + 1) * 2 * PACK]
                second = jnp.concatenate([second[:PACK], second[PACK:] * sign[i : i + 1]], axis=0)
                merged = jnp.where(near[i : i + 1], first, second).astype(jnp.bfloat16)
                cross[buffer, rows, i * stations : (i + 1) * stations] = merged
        following = jnp.concatenate(
            [data_ref[number, 4], data_ref[number + groups // 2, 4]], axis=1
        ).astype(jnp.float32)
        shared = pltpu.roll(following, low + 1, 1, stride=1, stride_axis=0)
        shared = jnp.where(column == own, -1.0, shared)
        hot = []
        for i in range(PACK):
            value = spread(shared[i : i + 1, :])
            hot.append(
                jnp.concatenate(
                    [
                        jnp.where(value == wanted[k : k + PACK], one, zero)
                        for k in range(0, bin_count, PACK)
                    ],
                    axis=0,
                )
            )
        total[...] += product_transposed(jnp.concatenate(hot, axis=1), cross[buffer])
    copies = out_ref.shape[0] // groups
    middle = BIN_DEV // 2
    for group in range(groups):
        upper = total[group * BIN_DEV : group * BIN_DEV + middle, :]
        lower = total[group * BIN_DEV + middle : (group + 1) * BIN_DEV, :]
        value = jnp.concatenate([upper, lower], axis=1)
        for k in range(copies):
            out_ref[group * copies + k] = value


def lag_kernel(data_ref, high_ref, low_ref, own_ref, swapped_ref, out_ref):
    lag = lax.axis_index("lag")
    sources = data_ref.shape[0]
    owned, blocks = out_ref.shape[0], out_ref.shape[1] // LANES
    lane = lax.broadcasted_iota(jnp.int32, (owned, LANES), 1)
    is_real = lane % (2 * PACK) < PACK
    is_first = lane[: owned // 2] < LANES // 2
    turned = [[] for _ in range(blocks)]
    for tile in range(sources // 2):
        first, second = data_ref[2 * tile], data_ref[2 * tile + 1]
        value = jnp.concatenate(
            [
                jnp.where(is_first, first, pltpu.roll(second, LANES // 2, 1)),
                jnp.where(is_first, pltpu.roll(first, LANES // 2, 1), second),
            ],
            axis=0,
        )
        partner = jnp.where(
            is_real, pltpu.roll(value, LANES - PACK, 1), pltpu.roll(value, PACK, 1)
        )
        at = slice(tile * LANES, (tile + 1) * LANES)
        for block in range(blocks):
            turned[block].append(
                value * own_ref[lag, block : block + 1, at]
                + partner * swapped_ref[lag, block : block + 1, at]
            )
    left = jnp.concatenate([jnp.concatenate(row, axis=1) for row in turned], axis=0)
    left_high, left_low = split_float(left)
    value = product(left_high, high_ref[...]) + product(left_low, high_ref[...])
    value = value + product(left_high, low_ref[...])
    for block in range(blocks):
        out_ref[:, block * LANES : (block + 1) * LANES] = value[block * owned : (block + 1) * owned]


def call(kernel, arrays, spaces, out_shape, scratch=()):
    arrays = [
        pltpu.with_memory_space_constraint(array, space) if space is pltpu.HBM else array
        for array, space in zip(arrays, spaces)
    ]
    return pl.pallas_call(
        kernel,
        in_specs=[pl.BlockSpec(memory_space=space) for space in spaces],
        out_specs=pl.BlockSpec(memory_space=pltpu.VMEM),
        out_shape=out_shape,
        scratch_shapes=list(scratch),
        compiler_params=pltpu.CompilerParams(vmem_limit_bytes=48 << 20),
    )(*arrays)


def local_by_frequency(waveforms, pair_bin):
    station_count, segments, _ = waveforms.shape
    groups = lax.axis_size("grp")
    lag_count = lax.axis_size("lag")
    freq_count = NFFT // 2 // lag_count
    stations = station_count * groups
    bin_count = BIN_DEV * groups
    rows = waveforms.reshape(station_count * segments, NFFT)
    small, tables = [jnp.asarray(t) for t in forward_constants(freq_count, lag_count)]
    whitened = call(
        whiten_kernel,
        [pair_bin, rows, small, tables],
        [pltpu.HBM] * 4,
        jax.ShapeDtypeStruct((groups, 5, PACK, LANES), jnp.bfloat16),
        [
            pltpu.VMEM(pair_bin.shape, jnp.int32),
            pltpu.VMEM(rows.shape, jnp.float32),
            pltpu.VMEM(small.shape[1:], jnp.float32),
            pltpu.VMEM(tables.shape, jnp.bfloat16),
            pltpu.VMEM((freq_count + LANES, freq_count), jnp.bfloat16),
            pltpu.VMEM((2, RADIX, station_count * segments, LANES), jnp.float32),
            pltpu.SemaphoreType.DMA((5,)),
        ],
    )
    received = lax.all_to_all(whitened, "grp", 0, 0, tiled=True)
    outgoing = call(
        pair_kernel,
        [received],
        [pltpu.VMEM],
        jax.ShapeDtypeStruct((groups * lag_count, BIN_DEV // 2, LANES), jnp.float32),
        [
            pltpu.VMEM((2, stations, 2 * LANES), jnp.bfloat16),
            pltpu.VMEM((2, 4 * PACK, PACK * stations), jnp.bfloat16),
            pltpu.VMEM((bin_count, 4 * PACK), jnp.float32),
        ],
    )
    owned = lax.all_to_all(outgoing, ("grp", "lag"), 0, 0, tiled=True)
    high, low, own, swapped = [
        jnp.asarray(t) for t in inverse_constants(freq_count, lag_count, groups)
    ]
    return call(
        lag_kernel,
        [owned, high, low, own, swapped],
        [pltpu.VMEM] * 5,
        jax.ShapeDtypeStruct((BIN_DEV, LAGS // lag_count), jnp.float32),
    )


def fits_by_frequency(mesh, waveforms):
    groups, lag_count = mesh.shape["grp"], mesh.shape["lag"]
    stations, segments, _ = waveforms.shape
    freq_count = NFFT // 2 // lag_count
    return (
        lag_count == 2
        and stations == groups * PACK == 2 * LANES
        and freq_count == RADIX * LANES
        and segments * 2 * (LANES // groups) == LANES
        and groups * BIN_DEV <= 256
    )


def solution(mesh):
    in_specs = (P("grp", None, None), P("grp", None))
    out_specs = P("grp", "lag")

    def run(waveforms, pair_bin):
        body = local_by_frequency if fits_by_frequency(mesh, waveforms) else local
        return jax.shard_map(
            body, mesh=mesh, in_specs=in_specs, out_specs=out_specs, check_vma=False
        )(waveforms, pair_bin)

    return run
```

```python
import math

import jax
import jax.numpy as jnp
import ml_dtypes
import numpy as np
from jax import lax
from jax.experimental import pallas as pl
from jax.experimental.pallas import tpu as pltpu
from jax.sharding import PartitionSpec as P

NFFT = 2048
LAGS = 1024
HW = 32
BIN_DEV = 8


EPSILON = 1e-06


def with_halo(block, sides, width):
    for axis, dim in sides:
        count = lax.axis_size(axis)
        forward = [(i, i + 1) for i in range(count - 1)]
        backward = [(target, source) for source, target in forward]
        low = lax.ppermute(
            lax.slice_in_dim(block, block.shape[dim] - width, None, axis=dim), axis, forward
        )
        high = lax.ppermute(lax.slice_in_dim(block, 0, width, axis=dim), axis, backward)
        block = jnp.concatenate([low, block, high], axis=dim)
    return block


def forward_table(freq_start, freq_count):
    sample_index = jnp.arange(NFFT, dtype=jnp.int32)[:, None]
    bin_index = freq_start + jnp.arange(freq_count, dtype=jnp.int32)[None, :]
    phase = (sample_index * bin_index % NFFT).astype(jnp.float32) * (2.0 * math.pi / NFFT)
    return jnp.concatenate([jnp.cos(phase), -jnp.sin(phase)], axis=1)


def inverse_table(freq_start, freq_count):
    bin_index = freq_start + jnp.arange(freq_count, dtype=jnp.int32)
    shifted = jnp.arange(LAGS, dtype=jnp.int32) - LAGS // 2
    phase = (bin_index[:, None] * shifted[None, :] % NFFT).astype(jnp.float32) * (
        2.0 * math.pi / NFFT
    )
    weight = jnp.where(bin_index == 0, 1.0, 2.0).astype(jnp.float32)[:, None] / NFFT
    return jnp.concatenate([weight * jnp.cos(phase), -weight * jnp.sin(phase)], axis=0)


def window_band(freq_count):
    padded_index = jnp.arange(freq_count + 2 * HW, dtype=jnp.int32)[:, None]
    bin_index = jnp.arange(freq_count, dtype=jnp.int32)[None, :]
    inside = (padded_index >= bin_index) & (padded_index <= bin_index + 2 * HW)
    return inside.astype(jnp.float32)


def window_count(freq_start, freq_count, half_length):
    bin_index = freq_start + jnp.arange(freq_count, dtype=jnp.int32)
    upper = jnp.minimum(bin_index + HW, half_length - 1)
    lower = jnp.maximum(bin_index - HW, 0)
    return (upper - lower + 1).astype(jnp.float32)


def add_block(running, whitened, remote, column_start, keep_pairs, imag_sign, pair_bin):
    freq_count = whitened.shape[2] // 2
    row_count = whitened.shape[0]
    column_count = remote.shape[0]
    own_real = whitened[..., :freq_count]
    own_imag = whitened[..., freq_count:]
    far_real = remote[..., :freq_count]
    far_imag = remote[..., freq_count:]
    own_stack = jnp.concatenate([own_real, own_imag], axis=1)
    own_alt = jnp.concatenate([own_real, -own_imag], axis=1)
    far_stack = jnp.concatenate([far_real, far_imag], axis=1)
    far_alt = jnp.concatenate([far_imag, far_real], axis=1)
    real_sum = jnp.einsum("asf,bsf->abf", own_stack, far_stack, preferred_element_type=jnp.float32)
    imag_sum = (
        jnp.einsum("asf,bsf->abf", own_alt, far_alt, preferred_element_type=jnp.float32) * imag_sign
    )
    cross = jnp.concatenate([real_sum, imag_sum], axis=2).astype(jnp.bfloat16)
    cross = cross.reshape(row_count * column_count, 2 * freq_count)
    block_bins = lax.dynamic_slice_in_dim(pair_bin, column_start, column_count, 1)
    block_bins = jnp.where(keep_pairs, block_bins, -1).reshape(-1)
    onehot = (block_bins[None, :] == jnp.arange(running.shape[0], dtype=jnp.int32)[:, None]).astype(
        jnp.bfloat16
    )
    return running + jnp.dot(onehot, cross, preferred_element_type=jnp.float32)


def local(waveforms, pair_bin):
    station_count = waveforms.shape[0]
    segments = waveforms.shape[1]
    groups = lax.axis_size("grp")
    group_index = lax.axis_index("grp")
    half_length = NFFT // 2
    freq_count = half_length // lax.axis_size("lag")
    freq_start = lax.axis_index("lag") * freq_count
    spectra = jnp.dot(
        waveforms.reshape(station_count * segments, NFFT),
        forward_table(freq_start, freq_count),
        precision=lax.Precision.HIGHEST,
        preferred_element_type=jnp.float32,
    )
    spectra = spectra.reshape(station_count, segments, 2 * freq_count)
    real_part = spectra[..., :freq_count]
    imag_part = spectra[..., freq_count:]
    amplitude = jnp.sqrt(real_part * real_part + imag_part * imag_part)
    padded = with_halo(amplitude, (("lag", 2),), HW)
    smoothed = jnp.dot(
        padded.reshape(station_count * segments, freq_count + 2 * HW),
        window_band(freq_count),
        precision=lax.Precision.HIGHEST,
        preferred_element_type=jnp.float32,
    )
    smoothed = smoothed.reshape(station_count, segments, freq_count) / window_count(
        freq_start, freq_count, half_length
    )
    whitened = jnp.concatenate(
        [real_part / (smoothed + EPSILON), imag_part / (smoothed + EPSILON)], axis=2
    ).astype(jnp.bfloat16)
    bins_total = BIN_DEV * groups
    row_start = group_index * station_count
    initial = jnp.zeros((bins_total, 2 * freq_count), jnp.float32)
    local_rows = jnp.arange(station_count, dtype=jnp.int32)
    remote = lax.all_gather(whitened, "grp", axis=0, tiled=True)
    group_total = remote.shape[0] // station_count
    per_step = max((divisor for divisor in (4, 3, 2, 1) if group_total % divisor == 0))
    step_count = group_total // per_step
    block_width = per_step * station_count
    blocks = remote.reshape(step_count, block_width, remote.shape[1], remote.shape[2])

    def one_step(step_index, carried):
        column_block = lax.dynamic_index_in_dim(blocks, step_index, 0, keepdims=False)
        column_start = step_index * block_width
        column_index = column_start + jnp.arange(block_width, dtype=jnp.int32)
        keep_pairs = column_index[None, :] > (row_start + local_rows)[:, None]

        def compute(accumulated):
            return add_block(
                accumulated, whitened, column_block, column_start, keep_pairs, 1.0, pair_bin
            )

        return lax.cond(
            column_start + block_width > row_start,
            compute,
            lambda accumulated: accumulated,
            carried,
        )

    binned = lax.fori_loop(0, step_count, one_step, initial)
    inverse = inverse_table(freq_start, freq_count)
    owned_bins = lax.psum_scatter(binned, "grp", scatter_dimension=0, tiled=True)
    lag_partial = jnp.dot(
        owned_bins, inverse, precision=lax.Precision.HIGHEST, preferred_element_type=jnp.float32
    )
    return lax.psum_scatter(lag_partial, "lag", scatter_dimension=1, tiled=True)


LANES = 128
RADIX = 4
SPLIT = NFFT // RADIX
PACK = 16


def halves(table):
    wide = np.asarray(table, np.float32)
    high = wide.astype(ml_dtypes.bfloat16)
    return high, (wide - high.astype(np.float32)).astype(ml_dtypes.bfloat16)


def forward_constants(freq_count, lag_count):
    steps = freq_count // RADIX
    sample = np.arange(SPLIT)
    width = HW // RADIX
    beyond = np.stack([steps + np.arange(width), np.arange(width) - width])
    beyond = beyond.reshape(-1)
    table = np.zeros((SPLIT, 2 * LANES))
    side = np.zeros((SPLIT, LANES))
    angle = 2.0 * np.pi / SPLIT * (sample[:, None] * np.arange(steps)[None, :] % SPLIT)
    table[:, :steps] = np.cos(angle)
    table[:, LANES : LANES + steps] = np.sin(angle)
    angle = 2.0 * np.pi / SPLIT * (sample[:, None] * beyond[None, :] % SPLIT)
    side[:, : beyond.size] = np.cos(angle)
    side[:, LANES // 2 : LANES // 2 + beyond.size] = np.sin(angle)
    tables = np.concatenate([*halves(table), halves(side)[0]], axis=1)
    order = np.concatenate([np.arange(steps) * RADIX + r for r in range(RADIX)])
    small = np.zeros((lag_count, 2 * RADIX + 8, freq_count), np.float32)
    for index in range(lag_count):
        start = index * freq_count
        for r in range(RADIX):
            angle = 2.0 * np.pi / NFFT * ((start + r) * sample % NFFT)
            small[index, 2 * r] = np.cos(angle)
            small[index, 2 * r + 1] = np.sin(angle)
        upper = np.minimum(start + order + HW, NFFT // 2 - 1)
        lower = np.maximum(start + order - HW, 0)
        small[index, 2 * RADIX] = 1.0 / (upper - lower + 1)
        small[index, 2 * RADIX + 1, :width] = index > 0
        small[index, 2 * RADIX + 1, LANES - width : LANES] = index < lag_count - 1
    return small, tables


def inverse_constants(freq_count, lag_count, groups):
    run = freq_count // groups
    quarter = run // RADIX
    index = np.arange(groups * lag_count)
    start = (index % lag_count) * freq_count + (index // lag_count) * run
    pair, half, step = np.meshgrid(np.arange(2), np.arange(2), np.arange(quarter), indexing="ij")
    offset = (RADIX * step + 2 * pair + half).reshape(2, PACK)
    bins = start[:, None, None] + offset[None]
    both = np.stack([bins, bins], axis=2)
    imaginary = np.stack([np.zeros_like(bins), np.ones_like(bins)], axis=2).reshape(-1)
    both = both.reshape(-1)
    angle = 2.0 * np.pi / NFFT * (both[:, None] * np.arange(LANES)[None, :] % NFFT)
    table = np.where(imaginary[:, None] == 1, -np.sin(angle), np.cos(angle))
    table_high, table_low = halves(table)
    lag_block = LAGS // lag_count
    weight = np.where(both == 0, 1.0, 2.0) / NFFT
    own, swapped = [], []
    for lag in range(lag_count):
        first = np.arange(lag_block // LANES) * LANES + lag * lag_block - LAGS // 2
        angle = 2.0 * np.pi / NFFT * (both[None, :] * first[:, None] % NFFT)
        own.append(weight * np.cos(angle))
        swapped.append(np.where(imaginary == 1, 1.0, -1.0) * weight * np.sin(angle))
    return (
        table_high,
        table_low,
        np.stack(own).astype(np.float32),
        np.stack(swapped).astype(np.float32),
    )


def split_float(value):
    high = value.astype(jnp.bfloat16)
    return high, (value - high.astype(jnp.float32)).astype(jnp.bfloat16)


def product(left, right):
    return jnp.dot(left, right, preferred_element_type=jnp.float32)


def product_transposed(left, right):
    return lax.dot_general(
        left, right, (((1,), (1,)), ((), ())), preferred_element_type=jnp.float32
    )


def whole_steps():
    reach = HW // RADIX
    row = lax.broadcasted_iota(jnp.int32, (2 * LANES, LANES), 0)
    column = lax.broadcasted_iota(jnp.int32, (2 * LANES, LANES), 1)
    beyond = row - LANES
    step = jnp.where(beyond < reach, beyond - reach, beyond + reach)
    step = jnp.where(row < LANES, row, step)
    inside = (row < LANES) | (beyond < reach) | (beyond >= LANES - reach)
    near = (jnp.abs(step - column) < reach) & inside
    return near.astype(jnp.float32).astype(jnp.bfloat16)


def whiten_kernel(
    bin_hbm, wave_hbm, small_hbm, table_hbm, out_ref,
    bin_ref, wave_ref, small_ref, table_ref, scratch, sems,
):
    rows = wave_ref.shape[0]
    segments = rows // PACK
    targets = out_ref.shape[0]
    moves = (
        (small_hbm.at[lax.axis_index("lag")], small_ref),
        (wave_hbm, wave_ref),
        (table_hbm, table_ref),
        (bin_hbm, bin_ref),
    )
    copies = [
        pltpu.make_async_copy(source, target, sems.at[k])
        for k, (source, target) in enumerate(moves)
    ]
    for copy in copies:
        copy.start()
    near = whole_steps()
    for copy in copies:
        copy.wait()
    quarter = [wave_ref[:, k * SPLIT : (k + 1) * SPLIT] for k in range(RADIX)]
    even_sum, odd_sum = quarter[0] + quarter[2], quarter[1] + quarter[3]
    even, odd = quarter[0] - quarter[2], quarter[1] - quarter[3]
    main, rest = slice(0, 2 * LANES), slice(2 * LANES, 4 * LANES)
    side = slice(4 * LANES, 5 * LANES)
    spectra, amplitudes, outside = [], [], []
    for r, first, second in (
        (0, even_sum + odd_sum, None), (1, even, -odd), (2, even_sum - odd_sum, None), (3, even, odd)
    ):
        cosine, sine = small_ref[2 * r : 2 * r + 1, :], small_ref[2 * r + 1 : 2 * r + 2, :]
        turned_real, turned_imag = first * cosine, -first * sine
        if second is not None:
            turned_real = turned_real + second * sine
            turned_imag = turned_imag + second * cosine
        high, low = split_float(jnp.concatenate([turned_real, turned_imag], axis=0))
        value = product(high, table_ref[:, main]) + product(low, table_ref[:, main])
        value = value + product(high, table_ref[:, rest])
        beyond = product(high, table_ref[:, side])
        real = value[:rows, :LANES] + value[rows:, LANES:]
        imag = value[rows:, :LANES] - value[:rows, LANES:]
        spectra.append((real, imag))
        amplitudes.append(jnp.sqrt(real * real + imag * imag))
        real = beyond[:rows] + pltpu.roll(beyond[rows:], LANES // 2, 1)
        imag = beyond[rows:] - pltpu.roll(beyond[:rows], LANES // 2, 1)
        outside.append(jnp.sqrt(real * real + imag * imag))
    reach = HW // RADIX
    there = small_ref[2 * RADIX + 1 : 2 * RADIX + 2, :LANES]
    outside = [pltpu.roll(value, LANES - reach, 1) * there for value in outside]
    sums = jnp.concatenate([sum(amplitudes), sum(outside)], axis=1)
    sums_high, sums_low = split_float(sums)
    common = product(sums_high, near) + product(sums_low, near)
    lane = lax.broadcasted_iota(jnp.int32, (rows, LANES), 1)
    for r, (real, imag) in enumerate(spectra):
        above = pltpu.roll(sum(amplitudes[: r + 1]), LANES - reach, 1)
        above = jnp.where(lane < LANES - reach, above, sum(outside[: r + 1]))
        below = pltpu.roll(sum(amplitudes[r:]), reach, 1)
        below = jnp.where(lane >= reach, below, sum(outside[r:]))
        count = small_ref[2 * RADIX : 2 * RADIX + 1, r * LANES : (r + 1) * LANES]
        scale = 1.0 / ((common + above + below) * count + EPSILON)
        scratch[0, r] = real * scale
        scratch[1, r] = imag * scale
    stations = bin_ref.shape[1]
    turned = pltpu.roll(
        bin_ref[...].astype(jnp.float32), (stations - lax.axis_index("grp") * PACK) % stations, 1
    )
    following = jnp.concatenate(
        [
            pltpu.roll(turned[i : i + 1, :], stations - 1 - i, 1)[:, : stations // 2]
            for i in range(PACK)
        ],
        axis=0,
    ).astype(jnp.bfloat16)
    width = LANES // targets
    chunk = lax.broadcasted_iota(jnp.int32, (PACK, LANES), 1) // width
    chunk = chunk.astype(jnp.float32).astype(jnp.bfloat16)
    masks = [chunk == jnp.bfloat16(place) for place in range(targets)]
    for pair in range(2):
        for part in range(2):
            rolled = []
            for half in range(2):
                for segment in range(segments):
                    rows_of = scratch[part, 2 * pair + half, pl.ds(segment, PACK, stride=segments), :]
                    shift = width * (half * segments + segment)
                    rows_of = pltpu.roll(rows_of, shift, 1) if shift else rows_of
                    rolled.append(rows_of.astype(jnp.bfloat16))
            for target in range(targets):
                value = rolled[-target % targets]
                for place in range(1, targets):
                    value = jnp.where(masks[place], rolled[(place - target) % targets], value)
                out_ref[target, 2 * pair + part] = value
    for target in range(targets):
        out_ref[target, 4] = following


def pair_kernel(data_ref, out_ref, spectra, cross, bins, total):
    groups = data_ref.shape[0]
    stations = groups * PACK
    bin_count = total.shape[0]
    width = LANES // groups
    half = stations // 2
    for group in range(groups):
        for pair in range(2):
            for part in range(2):
                spectra[
                    pair, group * PACK : (group + 1) * PACK, part * LANES : (part + 1) * LANES
                ] = data_ref[group, 2 * pair + part]
    station = lax.broadcasted_iota(jnp.int32, (half, half), 0)
    column = lax.broadcasted_iota(jnp.int32, (half, half), 1)
    for group in range(groups // 2):
        following = jnp.concatenate(
            [data_ref[group, 4], data_ref[group + groups // 2, 4]], axis=1
        ).astype(jnp.float32)
        bins[group * PACK : (group + 1) * PACK, :] = pltpu.roll(
            following, group * PACK + 1, 1, stride=1, stride_axis=0
        )
    near, far = bins[:, :half], bins[:, half:]
    inner = jnp.where(column > station, near, jnp.where(column < station, far.T, -1.0))
    bins[:, half:] = jnp.where(column <= station, far, near.T)
    bins[:, :half] = inner

    def spread(value):
        return jnp.broadcast_to(value, (PACK, value.shape[1])).astype(jnp.bfloat16)

    def swap(value):
        return jnp.concatenate([value[:, LANES:], value[:, :LANES]], axis=1)

    def as_float(mask):
        return jnp.where(mask, 1.0, 0.0)

    lane = lax.broadcasted_iota(jnp.int32, (PACK, 2 * LANES), 1)
    row = lax.broadcasted_iota(jnp.int32, (PACK, 2 * LANES), 0)
    place = (lane % LANES // width - lax.axis_index("grp") + groups) % groups
    slot = place // (groups // 2) * width + lane % width
    sign = jnp.where(lane < LANES, -1.0, 1.0)
    keep = as_float(slot == row)
    keep_own = keep.astype(jnp.bfloat16)
    keep_turned = (keep * sign).astype(jnp.bfloat16)
    folded = as_float(slot % (PACK // 2) == row % (PACK // 2))
    fold_own = jnp.where(row < PACK // 2, folded, 0.0).astype(jnp.bfloat16)
    fold_turned = jnp.where(row < PACK // 2, 0.0, -sign * folded).astype(jnp.bfloat16)
    first_bins = as_float(slot[:1] < PACK // 2).astype(jnp.bfloat16)
    last_bins = as_float(slot[:1] >= PACK // 2).astype(jnp.bfloat16)
    eight = PACK // 2
    for chunk in range(groups // 2):
        start = chunk * PACK
        for pair in range(2):
            own = spectra[pair, start : start + PACK, :].astype(jnp.float32)
            other = spectra[pair, half + start : half + start + PACK, :].astype(jnp.float32)
            upper, lower = [], []
            for i in range(PACK):
                value = spread(own[i : i + 1, :])
                upper += [value * keep_own, swap(value) * keep_turned]
                value = spread(other[i : i + 1, :])
                lower.append(value * fold_own + swap(value) * fold_turned)
            first = product_transposed(jnp.concatenate(upper, axis=0), spectra[pair])
            second_half = spectra[pair, half:, :]
            second = product_transposed(
                jnp.concatenate(lower, axis=0),
                jnp.concatenate([second_half * first_bins, second_half * last_bins], axis=0),
            )
            rows = slice(pair * 2 * PACK, (pair + 1) * 2 * PACK)
            for i in range(PACK):
                mine = first[i * 2 * PACK : (i + 1) * 2 * PACK]
                theirs = second[i * PACK : (i + 1) * PACK]
                theirs = jnp.concatenate(
                    [
                        theirs[:eight, :half],
                        theirs[:eight, half:],
                        theirs[eight:, :half],
                        theirs[eight:, half:],
                    ],
                    axis=0,
                )
                inner = jnp.where(column[:1] > start + i, mine[:, :half], theirs)
                at = i * stations
                cross[chunk, rows, at : at + half] = inner.astype(jnp.bfloat16)
                cross[chunk, rows, at + half : at + stations] = mine[:, half:].astype(jnp.bfloat16)
    wanted = lax.broadcasted_iota(jnp.int32, (bin_count, stations), 0).astype(jnp.float32)
    wanted = wanted.astype(jnp.bfloat16)
    one, zero = jnp.bfloat16(1), jnp.bfloat16(0)
    total[...] = jnp.zeros_like(total)
    for chunk in range(groups // 2):
        chunk_bins = bins[chunk * PACK : (chunk + 1) * PACK, :]
        hot = []
        for i in range(PACK):
            bin_row = spread(chunk_bins[i : i + 1, :])
            hot.append(
                jnp.concatenate(
                    [
                        jnp.where(bin_row == wanted[k : k + PACK], one, zero)
                        for k in range(0, bin_count, PACK)
                    ],
                    axis=0,
                )
            )
        total[...] += product_transposed(jnp.concatenate(hot, axis=1), cross[chunk])
    copies = out_ref.shape[0] // groups
    middle = BIN_DEV // 2
    for group in range(groups):
        upper = total[group * BIN_DEV : group * BIN_DEV + middle, :]
        lower = total[group * BIN_DEV + middle : (group + 1) * BIN_DEV, :]
        value = jnp.concatenate([upper, lower], axis=1)
        for k in range(copies):
            out_ref[group * copies + k] = value


def lag_kernel(data_ref, high_ref, low_ref, own_ref, swapped_ref, out_ref):
    lag = lax.axis_index("lag")
    sources = data_ref.shape[0]
    owned, blocks = out_ref.shape[0], out_ref.shape[1] // LANES
    lane = lax.broadcasted_iota(jnp.int32, (owned, LANES), 1)
    is_real = lane % (2 * PACK) < PACK
    is_first = lane[: owned // 2] < LANES // 2
    turned = [[] for _ in range(blocks)]
    for tile in range(sources // 2):
        first, second = data_ref[2 * tile], data_ref[2 * tile + 1]
        value = jnp.concatenate(
            [
                jnp.where(is_first, first, pltpu.roll(second, LANES // 2, 1)),
                jnp.where(is_first, pltpu.roll(first, LANES // 2, 1), second),
            ],
            axis=0,
        )
        partner = jnp.where(
            is_real, pltpu.roll(value, LANES - PACK, 1), pltpu.roll(value, PACK, 1)
        )
        at = slice(tile * LANES, (tile + 1) * LANES)
        for block in range(blocks):
            turned[block].append(
                value * own_ref[lag, block : block + 1, at]
                + partner * swapped_ref[lag, block : block + 1, at]
            )
    left = jnp.concatenate([jnp.concatenate(row, axis=1) for row in turned], axis=0)
    left_high, left_low = split_float(left)
    value = product(left_high, high_ref[...]) + product(left_low, high_ref[...])
    value = value + product(left_high, low_ref[...])
    for block in range(blocks):
        out_ref[:, block * LANES : (block + 1) * LANES] = value[block * owned : (block + 1) * owned]


def call(kernel, arrays, spaces, out_shape, scratch=()):
    arrays = [
        pltpu.with_memory_space_constraint(array, space) if space is pltpu.HBM else array
        for array, space in zip(arrays, spaces)
    ]
    return pl.pallas_call(
        kernel,
        in_specs=[pl.BlockSpec(memory_space=space) for space in spaces],
        out_specs=pl.BlockSpec(memory_space=pltpu.VMEM),
        out_shape=out_shape,
        scratch_shapes=list(scratch),
        compiler_params=pltpu.CompilerParams(vmem_limit_bytes=48 << 20),
    )(*arrays)


def local_by_frequency(waveforms, pair_bin):
    station_count, segments, _ = waveforms.shape
    groups = lax.axis_size("grp")
    lag_count = lax.axis_size("lag")
    freq_count = NFFT // 2 // lag_count
    stations = station_count * groups
    bin_count = BIN_DEV * groups
    rows = waveforms.reshape(station_count * segments, NFFT)
    small, tables = [jnp.asarray(t) for t in forward_constants(freq_count, lag_count)]
    whitened = call(
        whiten_kernel,
        [pair_bin, rows, small, tables],
        [pltpu.HBM] * 4,
        jax.ShapeDtypeStruct((groups, 5, PACK, LANES), jnp.bfloat16),
        [
            pltpu.VMEM(pair_bin.shape, jnp.int32),
            pltpu.VMEM(rows.shape, jnp.float32),
            pltpu.VMEM(small.shape[1:], jnp.float32),
            pltpu.VMEM(tables.shape, jnp.bfloat16),
            pltpu.VMEM((2, RADIX, station_count * segments, LANES), jnp.float32),
            pltpu.SemaphoreType.DMA((4,)),
        ],
    )
    received = lax.all_to_all(whitened, "grp", 0, 0, tiled=True)
    outgoing = call(
        pair_kernel,
        [received],
        [pltpu.VMEM],
        jax.ShapeDtypeStruct((groups * lag_count, BIN_DEV // 2, LANES), jnp.float32),
        [
            pltpu.VMEM((2, stations, 2 * LANES), jnp.bfloat16),
            pltpu.VMEM((groups // 2, 4 * PACK, PACK * stations), jnp.bfloat16),
            pltpu.VMEM((stations // 2, stations), jnp.float32),
            pltpu.VMEM((bin_count, 4 * PACK), jnp.float32),
        ],
    )
    owned = lax.all_to_all(outgoing, ("grp", "lag"), 0, 0, tiled=True)
    high, low, own, swapped = [
        jnp.asarray(t) for t in inverse_constants(freq_count, lag_count, groups)
    ]
    return call(
        lag_kernel,
        [owned, high, low, own, swapped],
        [pltpu.VMEM] * 5,
        jax.ShapeDtypeStruct((BIN_DEV, LAGS // lag_count), jnp.float32),
    )


def fits_by_frequency(mesh, waveforms):
    groups, lag_count = mesh.shape["grp"], mesh.shape["lag"]
    stations, segments, _ = waveforms.shape
    freq_count = NFFT // 2 // lag_count
    return (
        lag_count == 2
        and stations == groups * PACK == 2 * LANES
        and freq_count == RADIX * LANES
        and segments * 2 * (LANES // groups) == LANES
        and groups * BIN_DEV <= 256
    )


def solution(mesh):
    in_specs = (P("grp", None, None), P("grp", None))
    out_specs = P("grp", "lag")

    def run(waveforms, pair_bin):
        body = local_by_frequency if fits_by_frequency(mesh, waveforms) else local
        return jax.shard_map(
            body, mesh=mesh, in_specs=in_specs, out_specs=out_specs, check_vma=False
        )(waveforms, pair_bin)

    return run
```

```python
import math

import jax
import jax.numpy as jnp
import ml_dtypes
import numpy as np
from jax import lax
from jax.experimental import pallas as pl
from jax.experimental.pallas import tpu as pltpu
from jax.sharding import PartitionSpec as P

NFFT = 2048
LAGS = 1024
HW = 32
BIN_DEV = 8


EPSILON = 1e-06


def with_halo(block, sides, width):
    for axis, dim in sides:
        count = lax.axis_size(axis)
        forward = [(i, i + 1) for i in range(count - 1)]
        backward = [(target, source) for source, target in forward]
        low = lax.ppermute(
            lax.slice_in_dim(block, block.shape[dim] - width, None, axis=dim), axis, forward
        )
        high = lax.ppermute(lax.slice_in_dim(block, 0, width, axis=dim), axis, backward)
        block = jnp.concatenate([low, block, high], axis=dim)
    return block


def forward_table(freq_start, freq_count):
    sample_index = jnp.arange(NFFT, dtype=jnp.int32)[:, None]
    bin_index = freq_start + jnp.arange(freq_count, dtype=jnp.int32)[None, :]
    phase = (sample_index * bin_index % NFFT).astype(jnp.float32) * (2.0 * math.pi / NFFT)
    return jnp.concatenate([jnp.cos(phase), -jnp.sin(phase)], axis=1)


def inverse_table(freq_start, freq_count):
    bin_index = freq_start + jnp.arange(freq_count, dtype=jnp.int32)
    shifted = jnp.arange(LAGS, dtype=jnp.int32) - LAGS // 2
    phase = (bin_index[:, None] * shifted[None, :] % NFFT).astype(jnp.float32) * (
        2.0 * math.pi / NFFT
    )
    weight = jnp.where(bin_index == 0, 1.0, 2.0).astype(jnp.float32)[:, None] / NFFT
    return jnp.concatenate([weight * jnp.cos(phase), -weight * jnp.sin(phase)], axis=0)


def window_band(freq_count):
    padded_index = jnp.arange(freq_count + 2 * HW, dtype=jnp.int32)[:, None]
    bin_index = jnp.arange(freq_count, dtype=jnp.int32)[None, :]
    inside = (padded_index >= bin_index) & (padded_index <= bin_index + 2 * HW)
    return inside.astype(jnp.float32)


def window_count(freq_start, freq_count, half_length):
    bin_index = freq_start + jnp.arange(freq_count, dtype=jnp.int32)
    upper = jnp.minimum(bin_index + HW, half_length - 1)
    lower = jnp.maximum(bin_index - HW, 0)
    return (upper - lower + 1).astype(jnp.float32)


def add_block(running, whitened, remote, column_start, keep_pairs, imag_sign, pair_bin):
    freq_count = whitened.shape[2] // 2
    row_count = whitened.shape[0]
    column_count = remote.shape[0]
    own_real = whitened[..., :freq_count]
    own_imag = whitened[..., freq_count:]
    far_real = remote[..., :freq_count]
    far_imag = remote[..., freq_count:]
    own_stack = jnp.concatenate([own_real, own_imag], axis=1)
    own_alt = jnp.concatenate([own_real, -own_imag], axis=1)
    far_stack = jnp.concatenate([far_real, far_imag], axis=1)
    far_alt = jnp.concatenate([far_imag, far_real], axis=1)
    real_sum = jnp.einsum("asf,bsf->abf", own_stack, far_stack, preferred_element_type=jnp.float32)
    imag_sum = (
        jnp.einsum("asf,bsf->abf", own_alt, far_alt, preferred_element_type=jnp.float32) * imag_sign
    )
    cross = jnp.concatenate([real_sum, imag_sum], axis=2).astype(jnp.bfloat16)
    cross = cross.reshape(row_count * column_count, 2 * freq_count)
    block_bins = lax.dynamic_slice_in_dim(pair_bin, column_start, column_count, 1)
    block_bins = jnp.where(keep_pairs, block_bins, -1).reshape(-1)
    onehot = (block_bins[None, :] == jnp.arange(running.shape[0], dtype=jnp.int32)[:, None]).astype(
        jnp.bfloat16
    )
    return running + jnp.dot(onehot, cross, preferred_element_type=jnp.float32)


def local(waveforms, pair_bin):
    station_count = waveforms.shape[0]
    segments = waveforms.shape[1]
    groups = lax.axis_size("grp")
    group_index = lax.axis_index("grp")
    half_length = NFFT // 2
    freq_count = half_length // lax.axis_size("lag")
    freq_start = lax.axis_index("lag") * freq_count
    spectra = jnp.dot(
        waveforms.reshape(station_count * segments, NFFT),
        forward_table(freq_start, freq_count),
        precision=lax.Precision.HIGHEST,
        preferred_element_type=jnp.float32,
    )
    spectra = spectra.reshape(station_count, segments, 2 * freq_count)
    real_part = spectra[..., :freq_count]
    imag_part = spectra[..., freq_count:]
    amplitude = jnp.sqrt(real_part * real_part + imag_part * imag_part)
    padded = with_halo(amplitude, (("lag", 2),), HW)
    smoothed = jnp.dot(
        padded.reshape(station_count * segments, freq_count + 2 * HW),
        window_band(freq_count),
        precision=lax.Precision.HIGHEST,
        preferred_element_type=jnp.float32,
    )
    smoothed = smoothed.reshape(station_count, segments, freq_count) / window_count(
        freq_start, freq_count, half_length
    )
    whitened = jnp.concatenate(
        [real_part / (smoothed + EPSILON), imag_part / (smoothed + EPSILON)], axis=2
    ).astype(jnp.bfloat16)
    bins_total = BIN_DEV * groups
    row_start = group_index * station_count
    initial = jnp.zeros((bins_total, 2 * freq_count), jnp.float32)
    local_rows = jnp.arange(station_count, dtype=jnp.int32)
    remote = lax.all_gather(whitened, "grp", axis=0, tiled=True)
    group_total = remote.shape[0] // station_count
    per_step = max((divisor for divisor in (4, 3, 2, 1) if group_total % divisor == 0))
    step_count = group_total // per_step
    block_width = per_step * station_count
    blocks = remote.reshape(step_count, block_width, remote.shape[1], remote.shape[2])

    def one_step(step_index, carried):
        column_block = lax.dynamic_index_in_dim(blocks, step_index, 0, keepdims=False)
        column_start = step_index * block_width
        column_index = column_start + jnp.arange(block_width, dtype=jnp.int32)
        keep_pairs = column_index[None, :] > (row_start + local_rows)[:, None]

        def compute(accumulated):
            return add_block(
                accumulated, whitened, column_block, column_start, keep_pairs, 1.0, pair_bin
            )

        return lax.cond(
            column_start + block_width > row_start,
            compute,
            lambda accumulated: accumulated,
            carried,
        )

    binned = lax.fori_loop(0, step_count, one_step, initial)
    inverse = inverse_table(freq_start, freq_count)
    owned_bins = lax.psum_scatter(binned, "grp", scatter_dimension=0, tiled=True)
    lag_partial = jnp.dot(
        owned_bins, inverse, precision=lax.Precision.HIGHEST, preferred_element_type=jnp.float32
    )
    return lax.psum_scatter(lag_partial, "lag", scatter_dimension=1, tiled=True)


LANES = 128
RADIX = 4
SPLIT = NFFT // RADIX
PACK = 16


def halves(table):
    wide = np.asarray(table, np.float32)
    high = wide.astype(ml_dtypes.bfloat16)
    return high, (wide - high.astype(np.float32)).astype(ml_dtypes.bfloat16)


def forward_constants():
    steps = SPLIT // 2
    sample = np.arange(SPLIT)
    angle = 2.0 * np.pi / SPLIT * (sample[:, None] * np.arange(steps)[None, :] % SPLIT)
    table = np.concatenate([np.cos(angle), np.sin(angle)], axis=1)
    small = np.zeros((3 * RADIX, SPLIT), np.float32)
    for r in range(RADIX):
        angle = 2.0 * np.pi / NFFT * (r * sample % NFFT)
        small[2 * r] = np.cos(angle)
        small[2 * r + 1] = np.sin(angle)
        bins = RADIX * np.arange(steps) + r
        upper = np.minimum(bins + HW, NFFT // 2 - 1)
        lower = np.maximum(bins - HW, 0)
        small[2 * RADIX + r, :steps] = 1.0 / (upper - lower + 1)
    return small, np.concatenate(halves(table), axis=1)


def inverse_constants(freq_count, lag_count, groups):
    run = freq_count // groups
    quarter = run // RADIX
    index = np.arange(groups * lag_count)
    start = (index % lag_count) * freq_count + (index // lag_count) * run
    pair, half, step = np.meshgrid(np.arange(2), np.arange(2), np.arange(quarter), indexing="ij")
    offset = (RADIX * step + 2 * pair + half).reshape(2, PACK)
    bins = start[:, None, None] + offset[None]
    both = np.stack([bins, bins], axis=2)
    imaginary = np.stack([np.zeros_like(bins), np.ones_like(bins)], axis=2).reshape(-1)
    both = both.reshape(-1)
    angle = 2.0 * np.pi / NFFT * (both[:, None] * np.arange(LANES)[None, :] % NFFT)
    table = np.where(imaginary[:, None] == 1, -np.sin(angle), np.cos(angle))
    table_high, table_low = halves(table)
    lag_block = LAGS // lag_count
    weight = np.where(both == 0, 1.0, 2.0) / NFFT
    own, swapped = [], []
    for lag in range(lag_count):
        first = np.arange(lag_block // LANES) * LANES + lag * lag_block - LAGS // 2
        angle = 2.0 * np.pi / NFFT * (both[None, :] * first[:, None] % NFFT)
        own.append(weight * np.cos(angle))
        swapped.append(np.where(imaginary == 1, 1.0, -1.0) * weight * np.sin(angle))
    return (
        table_high,
        table_low,
        np.stack(own).astype(np.float32),
        np.stack(swapped).astype(np.float32),
    )


def split_float(value):
    high = value.astype(jnp.bfloat16)
    return high, (value - high.astype(jnp.float32)).astype(jnp.bfloat16)


def product(left, right):
    return jnp.dot(left, right, preferred_element_type=jnp.float32)


def product_transposed(left, right):
    return lax.dot_general(
        left, right, (((1,), (1,)), ((), ())), preferred_element_type=jnp.float32
    )


def whiten_kernel(
    bin_hbm, wave_hbm, small_hbm, table_hbm, out_ref,
    bin_ref, wave_ref, small_ref, table_ref, scratch, sems,
):
    rows = wave_ref.shape[0]
    owned = bin_ref.shape[0]
    segments = rows // owned
    lags = lax.axis_size("lag")
    targets = out_ref.shape[0] // lags
    lag = lax.axis_index("lag")
    moves = (
        (small_hbm, small_ref),
        (wave_hbm.at[pl.ds(lag * rows, rows)], wave_ref),
        (table_hbm, table_ref),
        (bin_hbm.at[pl.ds(lag * owned, owned)], bin_ref),
    )
    copies = [
        pltpu.make_async_copy(source, target, sems.at[k])
        for k, (source, target) in enumerate(moves)
    ]
    for copy in copies:
        copy.start()
    steps = table_ref.shape[1] // 4
    reach = HW // RADIX
    row = lax.broadcasted_iota(jnp.int32, (steps, steps), 0)
    column = lax.broadcasted_iota(jnp.int32, (steps, steps), 1)
    near = jnp.where(jnp.abs(row - column) < reach, 1.0, 0.0).astype(jnp.bfloat16)
    for copy in copies:
        copy.wait()
    quarter = [wave_ref[:, k * SPLIT : (k + 1) * SPLIT] for k in range(RADIX)]
    even_sum, odd_sum = quarter[0] + quarter[2], quarter[1] + quarter[3]
    even, odd = quarter[0] - quarter[2], quarter[1] - quarter[3]
    high, low = [], []
    for r, first, second in (
        (0, even_sum + odd_sum, None), (1, even, -odd), (2, even_sum - odd_sum, None), (3, even, odd)
    ):
        cosine, sine = small_ref[2 * r : 2 * r + 1, :], small_ref[2 * r + 1 : 2 * r + 2, :]
        turned_real, turned_imag = first * cosine, -first * sine
        if second is not None:
            turned_real = turned_real + second * sine
            turned_imag = turned_imag + second * cosine
        for turned in (turned_real, turned_imag):
            turned_high, turned_low = split_float(turned)
            high.append(turned_high)
            low.append(turned_low)
    high = jnp.concatenate(high, axis=0)
    low = jnp.concatenate(low, axis=0)
    table_high, table_low = table_ref[:, : 2 * steps], table_ref[:, 2 * steps :]
    value = product(high, table_high) + product(low, table_high) + product(high, table_low)
    spectra, amplitudes = [], []
    for r in range(RADIX):
        first = value[2 * r * rows : (2 * r + 1) * rows]
        second = value[(2 * r + 1) * rows : (2 * r + 2) * rows]
        real = first[:, :steps] + second[:, steps:]
        imag = second[:, :steps] - first[:, steps:]
        spectra.append((real, imag))
        amplitudes.append(jnp.sqrt(real * real + imag * imag))
    sums_high, sums_low = split_float(sum(amplitudes))
    common = product(sums_high, near) + product(sums_low, near)
    step = lax.broadcasted_iota(jnp.int32, (rows, steps), 1)
    for r, (real, imag) in enumerate(spectra):
        above = pltpu.roll(sum(amplitudes[: r + 1]), steps - reach, 1)
        above = jnp.where(step < steps - reach, above, 0.0)
        below = pltpu.roll(sum(amplitudes[r:]), reach, 1)
        below = jnp.where(step >= reach, below, 0.0)
        count = small_ref[2 * RADIX + r : 2 * RADIX + r + 1, :steps]
        scale = 1.0 / ((common + above + below) * count + EPSILON)
        for tile in range(lags):
            at = slice(tile * LANES, (tile + 1) * LANES)
            scratch[0, r, tile] = real[:, at] * scale[:, at]
            scratch[1, r, tile] = imag[:, at] * scale[:, at]
    stations = bin_ref.shape[1]
    first_station = lax.axis_index("grp") * PACK + lag * owned
    turned = pltpu.roll(
        bin_ref[...].astype(jnp.float32), (stations - first_station) % stations, 1
    )
    following = jnp.concatenate(
        [
            pltpu.roll(turned[i : i + 1, :], stations - 1 - i, 1)[:, : stations // 2]
            for i in range(owned)
        ],
        axis=0,
    ).astype(jnp.bfloat16)
    width = LANES // targets
    chunk = lax.broadcasted_iota(jnp.int32, (PACK, LANES), 1) // width
    bits = []
    while 2 ** len(bits) < targets:
        odd_chunk = chunk // 2 ** len(bits) % 2
        bits.append(odd_chunk.astype(jnp.float32).astype(jnp.bfloat16) == jnp.bfloat16(1))
    for pair in range(2):
        for tile in range(lags):
            tiles = []
            for half in range(2):
                for segment in range(segments):
                    at = pl.ds(segment, owned, stride=segments)
                    both = jnp.concatenate(
                        [scratch[part, 2 * pair + half, tile, at, :] for part in range(2)], axis=0
                    )
                    shift = width * (half * segments + segment)
                    both = pltpu.roll(both, shift, 1) if shift else both
                    tiles.append(both.astype(jnp.bfloat16))
            for bit, mask in enumerate(bits):
                tiles = [
                    jnp.where(mask, tiles[(k + 2**bit) % targets], tiles[k])
                    for k in range(targets)
                ]
            for target in range(targets):
                out_ref[target * lags + tile, pair * PACK : (pair + 1) * PACK, :] = tiles[
                    -target % targets
                ]
    for target in range(targets * lags):
        out_ref[target, 2 * PACK :, :] = following


def pair_kernel(data_ref, out_ref, spectra, cross, bins, total):
    groups = lax.axis_size("grp")
    stations = groups * PACK
    bin_count = total.shape[0]
    width = LANES // groups
    half = stations // 2
    shares = data_ref.shape[0] // groups
    owned = PACK // shares

    def gathered(group, first_row):
        return jnp.concatenate(
            [
                data_ref[group * shares + k, first_row : first_row + owned, :]
                for k in range(shares)
            ],
            axis=0,
        )

    for group in range(groups):
        for pair in range(2):
            for part in range(2):
                spectra[
                    pair, group * PACK : (group + 1) * PACK, part * LANES : (part + 1) * LANES
                ] = gathered(group, pair * PACK + part * owned)
    station = lax.broadcasted_iota(jnp.int32, (half, half), 0)
    column = lax.broadcasted_iota(jnp.int32, (half, half), 1)
    for group in range(groups // 2):
        following = jnp.concatenate(
            [gathered(group, 2 * PACK), gathered(group + groups // 2, 2 * PACK)], axis=1
        ).astype(jnp.float32)
        bins[group * PACK : (group + 1) * PACK, :] = pltpu.roll(
            following, group * PACK + 1, 1, stride=1, stride_axis=0
        )
    near, far = bins[:, :half], bins[:, half:]
    inner = jnp.where(column > station, near, jnp.where(column < station, far.T, -1.0))
    bins[:, half:] = jnp.where(column <= station, far, near.T)
    bins[:, :half] = inner

    def spread(value):
        return jnp.broadcast_to(value, (PACK, value.shape[1])).astype(jnp.bfloat16)

    def swap(value):
        return jnp.concatenate([value[:, LANES:], value[:, :LANES]], axis=1)

    def as_float(mask):
        return jnp.where(mask, 1.0, 0.0)

    lane = lax.broadcasted_iota(jnp.int32, (PACK, 2 * LANES), 1)
    row = lax.broadcasted_iota(jnp.int32, (PACK, 2 * LANES), 0)
    place = (lane % LANES // width - lax.axis_index("grp") + groups) % groups
    slot = place // (groups // 2) * width + lane % width
    sign = jnp.where(lane < LANES, -1.0, 1.0)
    keep = as_float(slot == row)
    keep_own = keep.astype(jnp.bfloat16)
    keep_turned = (keep * sign).astype(jnp.bfloat16)
    folded = as_float(slot % (PACK // 2) == row % (PACK // 2))
    fold_own = jnp.where(row < PACK // 2, folded, 0.0).astype(jnp.bfloat16)
    fold_turned = jnp.where(row < PACK // 2, 0.0, -sign * folded).astype(jnp.bfloat16)
    first_bins = as_float(slot[:1] < PACK // 2).astype(jnp.bfloat16)
    last_bins = as_float(slot[:1] >= PACK // 2).astype(jnp.bfloat16)
    eight = PACK // 2
    for chunk in range(groups // 2):
        start = chunk * PACK
        for pair in range(2):
            own = spectra[pair, start : start + PACK, :].astype(jnp.float32)
            other = spectra[pair, half + start : half + start + PACK, :].astype(jnp.float32)
            upper, lower = [], []
            for i in range(PACK):
                value = spread(own[i : i + 1, :])
                upper += [value * keep_own, swap(value) * keep_turned]
                value = spread(other[i : i + 1, :])
                lower.append(value * fold_own + swap(value) * fold_turned)
            first = product_transposed(jnp.concatenate(upper, axis=0), spectra[pair])
            second_half = spectra[pair, half:, :]
            second = product_transposed(
                jnp.concatenate(lower, axis=0),
                jnp.concatenate([second_half * first_bins, second_half * last_bins], axis=0),
            )
            rows = slice(pair * 2 * PACK, (pair + 1) * 2 * PACK)
            for i in range(PACK):
                mine = first[i * 2 * PACK : (i + 1) * 2 * PACK]
                theirs = second[i * PACK : (i + 1) * PACK]
                theirs = jnp.concatenate(
                    [
                        theirs[:eight, :half],
                        theirs[:eight, half:],
                        theirs[eight:, :half],
                        theirs[eight:, half:],
                    ],
                    axis=0,
                )
                inner = jnp.where(column[:1] > start + i, mine[:, :half], theirs)
                at = i * stations
                cross[chunk, rows, at : at + half] = inner.astype(jnp.bfloat16)
                cross[chunk, rows, at + half : at + stations] = mine[:, half:].astype(jnp.bfloat16)
    wanted = lax.broadcasted_iota(jnp.int32, (bin_count, stations), 0).astype(jnp.float32)
    wanted = wanted.astype(jnp.bfloat16)
    one, zero = jnp.bfloat16(1), jnp.bfloat16(0)
    total[...] = jnp.zeros_like(total)
    for chunk in range(groups // 2):
        chunk_bins = bins[chunk * PACK : (chunk + 1) * PACK, :]
        hot = []
        for i in range(PACK):
            bin_row = spread(chunk_bins[i : i + 1, :])
            hot.append(
                jnp.concatenate(
                    [
                        jnp.where(bin_row == wanted[k : k + PACK], one, zero)
                        for k in range(0, bin_count, PACK)
                    ],
                    axis=0,
                )
            )
        total[...] += product_transposed(jnp.concatenate(hot, axis=1), cross[chunk])
    copies = out_ref.shape[0] // groups
    middle = BIN_DEV // 2
    for group in range(groups):
        upper = total[group * BIN_DEV : group * BIN_DEV + middle, :]
        lower = total[group * BIN_DEV + middle : (group + 1) * BIN_DEV, :]
        value = jnp.concatenate([upper, lower], axis=1)
        for k in range(copies):
            out_ref[group * copies + k] = value


def lag_kernel(data_ref, high_ref, low_ref, own_ref, swapped_ref, out_ref):
    lag = lax.axis_index("lag")
    sources = data_ref.shape[0]
    owned, blocks = out_ref.shape[0], out_ref.shape[1] // LANES
    lane = lax.broadcasted_iota(jnp.int32, (owned, LANES), 1)
    is_real = lane % (2 * PACK) < PACK
    is_first = lane[: owned // 2] < LANES // 2
    turned = [[] for _ in range(blocks)]
    for tile in range(sources // 2):
        first, second = data_ref[2 * tile], data_ref[2 * tile + 1]
        value = jnp.concatenate(
            [
                jnp.where(is_first, first, pltpu.roll(second, LANES // 2, 1)),
                jnp.where(is_first, pltpu.roll(first, LANES // 2, 1), second),
            ],
            axis=0,
        )
        partner = jnp.where(
            is_real, pltpu.roll(value, LANES - PACK, 1), pltpu.roll(value, PACK, 1)
        )
        at = slice(tile * LANES, (tile + 1) * LANES)
        for block in range(blocks):
            turned[block].append(
                value * own_ref[lag, block : block + 1, at]
                + partner * swapped_ref[lag, block : block + 1, at]
            )
    left = jnp.concatenate([jnp.concatenate(row, axis=1) for row in turned], axis=0)
    left_high, left_low = split_float(left)
    value = product(left_high, high_ref[...]) + product(left_low, high_ref[...])
    value = value + product(left_high, low_ref[...])
    for block in range(blocks):
        out_ref[:, block * LANES : (block + 1) * LANES] = value[block * owned : (block + 1) * owned]


def call(kernel, arrays, spaces, out_shape, scratch=()):
    arrays = [
        pltpu.with_memory_space_constraint(array, space) if space is pltpu.HBM else array
        for array, space in zip(arrays, spaces)
    ]
    return pl.pallas_call(
        kernel,
        in_specs=[pl.BlockSpec(memory_space=space) for space in spaces],
        out_specs=pl.BlockSpec(memory_space=pltpu.VMEM),
        out_shape=out_shape,
        scratch_shapes=list(scratch),
        compiler_params=pltpu.CompilerParams(vmem_limit_bytes=48 << 20),
    )(*arrays)


def local_by_frequency(waveforms, pair_bin):
    station_count, segments, _ = waveforms.shape
    groups = lax.axis_size("grp")
    lag_count = lax.axis_size("lag")
    freq_count = NFFT // 2 // lag_count
    stations = station_count * groups
    bin_count = BIN_DEV * groups
    rows = waveforms.reshape(station_count * segments, NFFT)
    small, table = [jnp.asarray(t) for t in forward_constants()]
    owned = station_count // lag_count
    whitened = call(
        whiten_kernel,
        [pair_bin, rows, small, table],
        [pltpu.HBM] * 4,
        jax.ShapeDtypeStruct((groups * lag_count, 2 * PACK + owned, LANES), jnp.bfloat16),
        [
            pltpu.VMEM((owned, stations), jnp.int32),
            pltpu.VMEM((owned * segments, NFFT), jnp.float32),
            pltpu.VMEM(small.shape, jnp.float32),
            pltpu.VMEM(table.shape, jnp.bfloat16),
            pltpu.VMEM((2, RADIX, lag_count, owned * segments, LANES), jnp.float32),
            pltpu.SemaphoreType.DMA((4,)),
        ],
    )
    received = lax.all_to_all(whitened, ("grp", "lag"), 0, 0, tiled=True)
    outgoing = call(
        pair_kernel,
        [received],
        [pltpu.VMEM],
        jax.ShapeDtypeStruct((groups * lag_count, BIN_DEV // 2, LANES), jnp.float32),
        [
            pltpu.VMEM((2, stations, 2 * LANES), jnp.bfloat16),
            pltpu.VMEM((groups // 2, 4 * PACK, PACK * stations), jnp.bfloat16),
            pltpu.VMEM((stations // 2, stations), jnp.float32),
            pltpu.VMEM((bin_count, 4 * PACK), jnp.float32),
        ],
    )
    owned = lax.all_to_all(outgoing, ("grp", "lag"), 0, 0, tiled=True)
    high, low, own, swapped = [
        jnp.asarray(t) for t in inverse_constants(freq_count, lag_count, groups)
    ]
    return call(
        lag_kernel,
        [owned, high, low, own, swapped],
        [pltpu.VMEM] * 5,
        jax.ShapeDtypeStruct((BIN_DEV, LAGS // lag_count), jnp.float32),
    )


def fits_by_frequency(mesh, waveforms):
    groups, lag_count = mesh.shape["grp"], mesh.shape["lag"]
    stations, segments, _ = waveforms.shape
    freq_count = NFFT // 2 // lag_count
    return (
        lag_count == 2
        and stations == groups * PACK == 2 * LANES
        and freq_count == RADIX * LANES
        and segments * 2 * (LANES // groups) == LANES
        and groups * BIN_DEV <= 256
    )


def solution(mesh):
    in_specs = (P("grp", None, None), P("grp", None))
    out_specs = P("grp", "lag")

    def run(waveforms, pair_bin):
        body = local_by_frequency if fits_by_frequency(mesh, waveforms) else local
        return jax.shard_map(
            body, mesh=mesh, in_specs=in_specs, out_specs=out_specs, check_vma=False
        )(waveforms, pair_bin)

    return run
```

```python
import math

import jax
import jax.numpy as jnp
import ml_dtypes
import numpy as np
from jax import lax
from jax.experimental import pallas as pl
from jax.experimental.pallas import tpu as pltpu
from jax.sharding import PartitionSpec as P

NFFT = 2048
LAGS = 1024
HW = 32
BIN_DEV = 8


EPSILON = 1e-06


def with_halo(block, sides, width):
    for axis, dim in sides:
        count = lax.axis_size(axis)
        forward = [(i, i + 1) for i in range(count - 1)]
        backward = [(target, source) for source, target in forward]
        low = lax.ppermute(
            lax.slice_in_dim(block, block.shape[dim] - width, None, axis=dim), axis, forward
        )
        high = lax.ppermute(lax.slice_in_dim(block, 0, width, axis=dim), axis, backward)
        block = jnp.concatenate([low, block, high], axis=dim)
    return block


def forward_table(freq_start, freq_count):
    sample_index = jnp.arange(NFFT, dtype=jnp.int32)[:, None]
    bin_index = freq_start + jnp.arange(freq_count, dtype=jnp.int32)[None, :]
    phase = (sample_index * bin_index % NFFT).astype(jnp.float32) * (2.0 * math.pi / NFFT)
    return jnp.concatenate([jnp.cos(phase), -jnp.sin(phase)], axis=1)


def inverse_table(freq_start, freq_count):
    bin_index = freq_start + jnp.arange(freq_count, dtype=jnp.int32)
    shifted = jnp.arange(LAGS, dtype=jnp.int32) - LAGS // 2
    phase = (bin_index[:, None] * shifted[None, :] % NFFT).astype(jnp.float32) * (
        2.0 * math.pi / NFFT
    )
    weight = jnp.where(bin_index == 0, 1.0, 2.0).astype(jnp.float32)[:, None] / NFFT
    return jnp.concatenate([weight * jnp.cos(phase), -weight * jnp.sin(phase)], axis=0)


def window_band(freq_count):
    padded_index = jnp.arange(freq_count + 2 * HW, dtype=jnp.int32)[:, None]
    bin_index = jnp.arange(freq_count, dtype=jnp.int32)[None, :]
    inside = (padded_index >= bin_index) & (padded_index <= bin_index + 2 * HW)
    return inside.astype(jnp.float32)


def window_count(freq_start, freq_count, half_length):
    bin_index = freq_start + jnp.arange(freq_count, dtype=jnp.int32)
    upper = jnp.minimum(bin_index + HW, half_length - 1)
    lower = jnp.maximum(bin_index - HW, 0)
    return (upper - lower + 1).astype(jnp.float32)


def add_block(running, whitened, remote, column_start, keep_pairs, imag_sign, pair_bin):
    freq_count = whitened.shape[2] // 2
    row_count = whitened.shape[0]
    column_count = remote.shape[0]
    own_real = whitened[..., :freq_count]
    own_imag = whitened[..., freq_count:]
    far_real = remote[..., :freq_count]
    far_imag = remote[..., freq_count:]
    own_stack = jnp.concatenate([own_real, own_imag], axis=1)
    own_alt = jnp.concatenate([own_real, -own_imag], axis=1)
    far_stack = jnp.concatenate([far_real, far_imag], axis=1)
    far_alt = jnp.concatenate([far_imag, far_real], axis=1)
    real_sum = jnp.einsum("asf,bsf->abf", own_stack, far_stack, preferred_element_type=jnp.float32)
    imag_sum = (
        jnp.einsum("asf,bsf->abf", own_alt, far_alt, preferred_element_type=jnp.float32) * imag_sign
    )
    cross = jnp.concatenate([real_sum, imag_sum], axis=2).astype(jnp.bfloat16)
    cross = cross.reshape(row_count * column_count, 2 * freq_count)
    block_bins = lax.dynamic_slice_in_dim(pair_bin, column_start, column_count, 1)
    block_bins = jnp.where(keep_pairs, block_bins, -1).reshape(-1)
    onehot = (block_bins[None, :] == jnp.arange(running.shape[0], dtype=jnp.int32)[:, None]).astype(
        jnp.bfloat16
    )
    return running + jnp.dot(onehot, cross, preferred_element_type=jnp.float32)


def local(waveforms, pair_bin):
    station_count = waveforms.shape[0]
    segments = waveforms.shape[1]
    groups = lax.axis_size("grp")
    group_index = lax.axis_index("grp")
    half_length = NFFT // 2
    freq_count = half_length // lax.axis_size("lag")
    freq_start = lax.axis_index("lag") * freq_count
    spectra = jnp.dot(
        waveforms.reshape(station_count * segments, NFFT),
        forward_table(freq_start, freq_count),
        precision=lax.Precision.HIGHEST,
        preferred_element_type=jnp.float32,
    )
    spectra = spectra.reshape(station_count, segments, 2 * freq_count)
    real_part = spectra[..., :freq_count]
    imag_part = spectra[..., freq_count:]
    amplitude = jnp.sqrt(real_part * real_part + imag_part * imag_part)
    padded = with_halo(amplitude, (("lag", 2),), HW)
    smoothed = jnp.dot(
        padded.reshape(station_count * segments, freq_count + 2 * HW),
        window_band(freq_count),
        precision=lax.Precision.HIGHEST,
        preferred_element_type=jnp.float32,
    )
    smoothed = smoothed.reshape(station_count, segments, freq_count) / window_count(
        freq_start, freq_count, half_length
    )
    whitened = jnp.concatenate(
        [real_part / (smoothed + EPSILON), imag_part / (smoothed + EPSILON)], axis=2
    ).astype(jnp.bfloat16)
    bins_total = BIN_DEV * groups
    row_start = group_index * station_count
    initial = jnp.zeros((bins_total, 2 * freq_count), jnp.float32)
    local_rows = jnp.arange(station_count, dtype=jnp.int32)
    remote = lax.all_gather(whitened, "grp", axis=0, tiled=True)
    group_total = remote.shape[0] // station_count
    per_step = max((divisor for divisor in (4, 3, 2, 1) if group_total % divisor == 0))
    step_count = group_total // per_step
    block_width = per_step * station_count
    blocks = remote.reshape(step_count, block_width, remote.shape[1], remote.shape[2])

    def one_step(step_index, carried):
        column_block = lax.dynamic_index_in_dim(blocks, step_index, 0, keepdims=False)
        column_start = step_index * block_width
        column_index = column_start + jnp.arange(block_width, dtype=jnp.int32)
        keep_pairs = column_index[None, :] > (row_start + local_rows)[:, None]

        def compute(accumulated):
            return add_block(
                accumulated, whitened, column_block, column_start, keep_pairs, 1.0, pair_bin
            )

        return lax.cond(
            column_start + block_width > row_start,
            compute,
            lambda accumulated: accumulated,
            carried,
        )

    binned = lax.fori_loop(0, step_count, one_step, initial)
    inverse = inverse_table(freq_start, freq_count)
    owned_bins = lax.psum_scatter(binned, "grp", scatter_dimension=0, tiled=True)
    lag_partial = jnp.dot(
        owned_bins, inverse, precision=lax.Precision.HIGHEST, preferred_element_type=jnp.float32
    )
    return lax.psum_scatter(lag_partial, "lag", scatter_dimension=1, tiled=True)


LANES = 128
RADIX = 8
SPLIT = NFFT // RADIX
PACK = 16


def halves(table):
    wide = np.asarray(table, np.float32)
    high = wide.astype(ml_dtypes.bfloat16)
    return high, (wide - high.astype(np.float32)).astype(ml_dtypes.bfloat16)


def forward_constants():
    steps = SPLIT // 2
    sample = np.arange(SPLIT)
    angle = 2.0 * np.pi / SPLIT * (sample[:, None] * np.arange(steps)[None, :] % SPLIT)
    table = np.concatenate([np.cos(angle), np.sin(angle)], axis=1)
    small = np.zeros((3 * RADIX, SPLIT), np.float32)
    for r in range(RADIX):
        angle = 2.0 * np.pi / NFFT * (r * sample % NFFT)
        small[2 * r] = np.cos(angle)
        small[2 * r + 1] = np.sin(angle)
        bins = RADIX * np.arange(steps) + r
        upper = np.minimum(bins + HW, NFFT // 2 - 1)
        lower = np.maximum(bins - HW, 0)
        small[2 * RADIX + r, :steps] = 1.0 / (upper - lower + 1)
    return small, np.concatenate(halves(table), axis=1)


def inverse_constants(lag_count, groups):
    run = NFFT // 2 // (groups * lag_count)
    start = np.arange(groups * lag_count) * run
    pair, half, step = np.meshgrid(
        np.arange(2), np.arange(RADIX // 2), np.arange(run // RADIX), indexing="ij"
    )
    offset = (RADIX * step + RADIX // 2 * pair + half).reshape(2, PACK)
    bins = start[:, None, None] + offset[None]
    both = np.stack([bins, bins], axis=2)
    imaginary = np.stack([np.zeros_like(bins), np.ones_like(bins)], axis=2).reshape(-1)
    both = both.reshape(-1)
    angle = 2.0 * np.pi / NFFT * (both[:, None] * np.arange(LANES)[None, :] % NFFT)
    table = np.where(imaginary[:, None] == 1, -np.sin(angle), np.cos(angle))
    table_high, table_low = halves(table)
    lag_block = LAGS // lag_count
    weight = np.where(both == 0, 1.0, 2.0) / NFFT
    own, swapped = [], []
    for lag in range(lag_count):
        first = np.arange(lag_block // LANES) * LANES + lag * lag_block - LAGS // 2
        angle = 2.0 * np.pi / NFFT * (both[None, :] * first[:, None] % NFFT)
        own.append(weight * np.cos(angle))
        swapped.append(np.where(imaginary == 1, 1.0, -1.0) * weight * np.sin(angle))
    return (
        table_high,
        table_low,
        np.stack(own).astype(np.float32),
        np.stack(swapped).astype(np.float32),
    )


def split_float(value):
    high = value.astype(jnp.bfloat16)
    return high, (value - high.astype(jnp.float32)).astype(jnp.bfloat16)


def product(left, right):
    return jnp.dot(left, right, preferred_element_type=jnp.float32)


def product_transposed(left, right):
    return lax.dot_general(
        left, right, (((1,), (1,)), ((), ())), preferred_element_type=jnp.float32
    )


def whiten_kernel(
    bin_hbm, wave_hbm, small_hbm, table_hbm, out_ref,
    bin_ref, wave_ref, small_ref, table_ref, scratch, sems,
):
    rows = wave_ref.shape[0]
    owned = bin_ref.shape[0]
    segments = rows // owned
    targets = out_ref.shape[0]
    lag = lax.axis_index("lag")
    moves = (
        (small_hbm, small_ref),
        (wave_hbm.at[pl.ds(lag * rows, rows)], wave_ref),
        (table_hbm, table_ref),
        (bin_hbm.at[pl.ds(lag * owned, owned)], bin_ref),
    )
    copies = [
        pltpu.make_async_copy(source, target, sems.at[k])
        for k, (source, target) in enumerate(moves)
    ]
    for copy in copies:
        copy.start()
    steps = table_ref.shape[1] // 4
    reach = HW // RADIX
    row = lax.broadcasted_iota(jnp.int32, (steps, steps), 0)
    column = lax.broadcasted_iota(jnp.int32, (steps, steps), 1)
    near = jnp.where(jnp.abs(row - column) < reach, 1.0, 0.0).astype(jnp.bfloat16)
    for copy in copies:
        copy.wait()
    part = [wave_ref[:, k * SPLIT : (k + 1) * SPLIT] for k in range(RADIX)]
    sums = [part[k] + part[k + 4] for k in range(4)]
    gaps = [part[k] - part[k + 4] for k in range(4)]
    even, odd = sums[0] + sums[2], sums[1] + sums[3]
    even_gap, odd_gap = sums[0] - sums[2], sums[1] - sums[3]
    across, along = math.sqrt(0.5) * (gaps[1] - gaps[3]), math.sqrt(0.5) * (gaps[1] + gaps[3])
    folded = (
        (even + odd, None),
        (gaps[0] + across, -gaps[2] - along),
        (even_gap, -odd_gap),
        (gaps[0] - across, gaps[2] - along),
        (even - odd, None),
        (gaps[0] - across, along - gaps[2]),
        (even_gap, odd_gap),
        (gaps[0] + across, gaps[2] + along),
    )
    high, low = [], []
    for r, (first, second) in enumerate(folded):
        cosine, sine = small_ref[2 * r : 2 * r + 1, :], small_ref[2 * r + 1 : 2 * r + 2, :]
        turned_real, turned_imag = first * cosine, -first * sine
        if second is not None:
            turned_real = turned_real + second * sine
            turned_imag = turned_imag + second * cosine
        for turned in (turned_real, turned_imag):
            turned_high, turned_low = split_float(turned)
            high.append(turned_high)
            low.append(turned_low)
    high = jnp.concatenate(high, axis=0)
    low = jnp.concatenate(low, axis=0)
    table_high, table_low = table_ref[:, : 2 * steps], table_ref[:, 2 * steps :]
    value = product(high, table_high) + product(low, table_high) + product(high, table_low)
    spectra, amplitudes = [], []
    for r in range(RADIX):
        first = value[2 * r * rows : (2 * r + 1) * rows]
        second = value[(2 * r + 1) * rows : (2 * r + 2) * rows]
        real = first[:, :steps] + second[:, steps:]
        imag = second[:, :steps] - first[:, steps:]
        spectra.append((real, imag))
        amplitudes.append(jnp.sqrt(real * real + imag * imag))
    sums_high, sums_low = split_float(sum(amplitudes))
    common = product(sums_high, near) + product(sums_low, near)
    step = lax.broadcasted_iota(jnp.int32, (rows, steps), 1)
    for r, (real, imag) in enumerate(spectra):
        above = pltpu.roll(sum(amplitudes[: r + 1]), steps - reach, 1)
        above = jnp.where(step < steps - reach, above, 0.0)
        below = pltpu.roll(sum(amplitudes[r:]), reach, 1)
        below = jnp.where(step >= reach, below, 0.0)
        count = small_ref[2 * RADIX + r : 2 * RADIX + r + 1, :steps]
        scale = 1.0 / ((common + above + below) * count + EPSILON)
        scratch[0, r] = real * scale
        scratch[1, r] = imag * scale
    stations = bin_ref.shape[1]
    first_station = lax.axis_index("grp") * PACK + lag * owned
    turned = pltpu.roll(
        bin_ref[...].astype(jnp.float32), (stations - first_station) % stations, 1
    )
    following = jnp.concatenate(
        [
            pltpu.roll(turned[i : i + 1, :], stations - 1 - i, 1)[:, : stations // 2]
            for i in range(owned)
        ],
        axis=0,
    ).astype(jnp.bfloat16)
    width = LANES // targets
    chunk = lax.broadcasted_iota(jnp.int32, (PACK, LANES), 1) // width
    bits = []
    while 2 ** len(bits) < targets:
        odd_chunk = chunk // 2 ** len(bits) % 2
        bits.append(odd_chunk.astype(jnp.float32).astype(jnp.bfloat16) == jnp.bfloat16(1))
    for pair in range(2):
        tiles = []
        for half in range(RADIX // 2):
            for segment in range(segments):
                at = pl.ds(segment, owned, stride=segments)
                both = jnp.concatenate(
                    [scratch[k, RADIX // 2 * pair + half, at, :] for k in range(2)], axis=0
                )
                shift = width * (half * segments + segment)
                both = pltpu.roll(both, shift, 1) if shift else both
                tiles.append(both.astype(jnp.bfloat16))
        for bit, mask in enumerate(bits):
            tiles = [
                jnp.where(mask, tiles[(k + 2**bit) % targets], tiles[k]) for k in range(targets)
            ]
        for target in range(targets):
            out_ref[target, pair * PACK : (pair + 1) * PACK, :] = tiles[-target % targets]
    for target in range(targets):
        out_ref[target, 2 * PACK :, :] = following


def pair_kernel(data_ref, out_ref, spectra, cross, bins, total):
    groups = lax.axis_size("grp")
    stations = groups * PACK
    bin_count = total.shape[0]
    width = LANES // data_ref.shape[0]
    half = stations // 2
    shares = data_ref.shape[0] // groups
    owned = PACK // shares

    def gathered(group, first_row):
        return jnp.concatenate(
            [
                data_ref[group * shares + k, first_row : first_row + owned, :]
                for k in range(shares)
            ],
            axis=0,
        )

    for group in range(groups):
        for pair in range(2):
            for part in range(2):
                spectra[
                    pair, group * PACK : (group + 1) * PACK, part * LANES : (part + 1) * LANES
                ] = gathered(group, pair * PACK + part * owned)
    station = lax.broadcasted_iota(jnp.int32, (half, half), 0)
    column = lax.broadcasted_iota(jnp.int32, (half, half), 1)
    for group in range(groups // 2):
        following = jnp.concatenate(
            [gathered(group, 2 * PACK), gathered(group + groups // 2, 2 * PACK)], axis=1
        ).astype(jnp.float32)
        bins[group * PACK : (group + 1) * PACK, :] = pltpu.roll(
            following, group * PACK + 1, 1, stride=1, stride_axis=0
        )
    near, far = bins[:, :half], bins[:, half:]
    inner = jnp.where(column > station, near, jnp.where(column < station, far.T, -1.0))
    bins[:, half:] = jnp.where(column <= station, far, near.T)
    bins[:, :half] = inner

    def spread(value):
        return jnp.broadcast_to(value, (PACK, value.shape[1])).astype(jnp.bfloat16)

    def swap(value):
        return jnp.concatenate([value[:, LANES:], value[:, :LANES]], axis=1)

    def as_float(mask):
        return jnp.where(mask, 1.0, 0.0)

    lane = lax.broadcasted_iota(jnp.int32, (PACK, 2 * LANES), 1)
    row = lax.broadcasted_iota(jnp.int32, (PACK, 2 * LANES), 0)
    position = lax.axis_index("grp") * shares + lax.axis_index("lag")
    place = (lane % LANES // width - position + shares * groups) % (shares * groups)
    slot = place // (LANES // PACK) * width + lane % width
    sign = jnp.where(lane < LANES, -1.0, 1.0)
    keep = as_float(slot == row)
    keep_own = keep.astype(jnp.bfloat16)
    keep_turned = (keep * sign).astype(jnp.bfloat16)
    folded = as_float(slot % (PACK // 2) == row % (PACK // 2))
    fold_own = jnp.where(row < PACK // 2, folded, 0.0).astype(jnp.bfloat16)
    fold_turned = jnp.where(row < PACK // 2, 0.0, -sign * folded).astype(jnp.bfloat16)
    first_bins = as_float(slot[:1] < PACK // 2).astype(jnp.bfloat16)
    last_bins = as_float(slot[:1] >= PACK // 2).astype(jnp.bfloat16)
    eight = PACK // 2
    for chunk in range(groups // 2):
        start = chunk * PACK
        for pair in range(2):
            own = spectra[pair, start : start + PACK, :].astype(jnp.float32)
            other = spectra[pair, half + start : half + start + PACK, :].astype(jnp.float32)
            upper, lower = [], []
            for i in range(PACK):
                value = spread(own[i : i + 1, :])
                upper += [value * keep_own, swap(value) * keep_turned]
                value = spread(other[i : i + 1, :])
                lower.append(value * fold_own + swap(value) * fold_turned)
            first = product_transposed(jnp.concatenate(upper, axis=0), spectra[pair])
            second_half = spectra[pair, half:, :]
            second = product_transposed(
                jnp.concatenate(lower, axis=0),
                jnp.concatenate([second_half * first_bins, second_half * last_bins], axis=0),
            )
            rows = slice(pair * 2 * PACK, (pair + 1) * 2 * PACK)
            for i in range(PACK):
                mine = first[i * 2 * PACK : (i + 1) * 2 * PACK]
                theirs = second[i * PACK : (i + 1) * PACK]
                theirs = jnp.concatenate(
                    [
                        theirs[:eight, :half],
                        theirs[:eight, half:],
                        theirs[eight:, :half],
                        theirs[eight:, half:],
                    ],
                    axis=0,
                )
                inner = jnp.where(column[:1] > start + i, mine[:, :half], theirs)
                at = i * stations
                cross[chunk, rows, at : at + half] = inner.astype(jnp.bfloat16)
                cross[chunk, rows, at + half : at + stations] = mine[:, half:].astype(jnp.bfloat16)
    wanted = lax.broadcasted_iota(jnp.int32, (bin_count, stations), 0).astype(jnp.float32)
    wanted = wanted.astype(jnp.bfloat16)
    one, zero = jnp.bfloat16(1), jnp.bfloat16(0)
    total[...] = jnp.zeros_like(total)
    for chunk in range(groups // 2):
        chunk_bins = bins[chunk * PACK : (chunk + 1) * PACK, :]
        hot = []
        for i in range(PACK):
            bin_row = spread(chunk_bins[i : i + 1, :])
            hot.append(
                jnp.concatenate(
                    [
                        jnp.where(bin_row == wanted[k : k + PACK], one, zero)
                        for k in range(0, bin_count, PACK)
                    ],
                    axis=0,
                )
            )
        total[...] += product_transposed(jnp.concatenate(hot, axis=1), cross[chunk])
    copies = out_ref.shape[0] // groups
    middle = BIN_DEV // 2
    for group in range(groups):
        upper = total[group * BIN_DEV : group * BIN_DEV + middle, :]
        lower = total[group * BIN_DEV + middle : (group + 1) * BIN_DEV, :]
        value = jnp.concatenate([upper, lower], axis=1)
        for k in range(copies):
            out_ref[group * copies + k] = value


def lag_kernel(data_ref, high_ref, low_ref, own_ref, swapped_ref, out_ref):
    lag = lax.axis_index("lag")
    sources = data_ref.shape[0]
    owned, blocks = out_ref.shape[0], out_ref.shape[1] // LANES
    lane = lax.broadcasted_iota(jnp.int32, (owned, LANES), 1)
    is_real = lane % (2 * PACK) < PACK
    is_first = lane[: owned // 2] < LANES // 2
    turned = [[] for _ in range(blocks)]
    for tile in range(sources // 2):
        first, second = data_ref[2 * tile], data_ref[2 * tile + 1]
        value = jnp.concatenate(
            [
                jnp.where(is_first, first, pltpu.roll(second, LANES // 2, 1)),
                jnp.where(is_first, pltpu.roll(first, LANES // 2, 1), second),
            ],
            axis=0,
        )
        partner = jnp.where(
            is_real, pltpu.roll(value, LANES - PACK, 1), pltpu.roll(value, PACK, 1)
        )
        at = slice(tile * LANES, (tile + 1) * LANES)
        for block in range(blocks):
            turned[block].append(
                value * own_ref[lag, block : block + 1, at]
                + partner * swapped_ref[lag, block : block + 1, at]
            )
    left = jnp.concatenate([jnp.concatenate(row, axis=1) for row in turned], axis=0)
    left_high, left_low = split_float(left)
    value = product(left_high, high_ref[...]) + product(left_low, high_ref[...])
    value = value + product(left_high, low_ref[...])
    for block in range(blocks):
        out_ref[:, block * LANES : (block + 1) * LANES] = value[block * owned : (block + 1) * owned]


def call(kernel, arrays, spaces, out_shape, scratch=()):
    arrays = [
        pltpu.with_memory_space_constraint(array, space) if space is pltpu.HBM else array
        for array, space in zip(arrays, spaces)
    ]
    return pl.pallas_call(
        kernel,
        in_specs=[pl.BlockSpec(memory_space=space) for space in spaces],
        out_specs=pl.BlockSpec(memory_space=pltpu.VMEM),
        out_shape=out_shape,
        scratch_shapes=list(scratch),
        compiler_params=pltpu.CompilerParams(vmem_limit_bytes=48 << 20),
    )(*arrays)


def local_by_frequency(waveforms, pair_bin):
    station_count, segments, _ = waveforms.shape
    groups = lax.axis_size("grp")
    lag_count = lax.axis_size("lag")
    stations = station_count * groups
    bin_count = BIN_DEV * groups
    rows = waveforms.reshape(station_count * segments, NFFT)
    small, table = [jnp.asarray(t) for t in forward_constants()]
    owned = station_count // lag_count
    whitened = call(
        whiten_kernel,
        [pair_bin, rows, small, table],
        [pltpu.HBM] * 4,
        jax.ShapeDtypeStruct((groups * lag_count, 2 * PACK + owned, LANES), jnp.bfloat16),
        [
            pltpu.VMEM((owned, stations), jnp.int32),
            pltpu.VMEM((owned * segments, NFFT), jnp.float32),
            pltpu.VMEM(small.shape, jnp.float32),
            pltpu.VMEM(table.shape, jnp.bfloat16),
            pltpu.VMEM((2, RADIX, owned * segments, LANES), jnp.float32),
            pltpu.SemaphoreType.DMA((4,)),
        ],
    )
    received = lax.all_to_all(whitened, ("grp", "lag"), 0, 0, tiled=True)
    outgoing = call(
        pair_kernel,
        [received],
        [pltpu.VMEM],
        jax.ShapeDtypeStruct((groups * lag_count, BIN_DEV // 2, LANES), jnp.float32),
        [
            pltpu.VMEM((2, stations, 2 * LANES), jnp.bfloat16),
            pltpu.VMEM((groups // 2, 4 * PACK, PACK * stations), jnp.bfloat16),
            pltpu.VMEM((stations // 2, stations), jnp.float32),
            pltpu.VMEM((bin_count, 4 * PACK), jnp.float32),
        ],
    )
    owned = lax.all_to_all(outgoing, ("grp", "lag"), 0, 0, tiled=True)
    high, low, own, swapped = [
        jnp.asarray(t) for t in inverse_constants(lag_count, groups)
    ]
    return call(
        lag_kernel,
        [owned, high, low, own, swapped],
        [pltpu.VMEM] * 5,
        jax.ShapeDtypeStruct((BIN_DEV, LAGS // lag_count), jnp.float32),
    )


def fits_by_frequency(mesh, waveforms):
    groups, lag_count = mesh.shape["grp"], mesh.shape["lag"]
    stations, segments, _ = waveforms.shape
    return (
        lag_count == 2
        and stations == groups * PACK == 2 * LANES
        and segments * PACK == LANES
        and groups * lag_count * 2 * PACK == NFFT // 2 == RADIX * LANES
        and groups * BIN_DEV <= 256
    )


def solution(mesh):
    in_specs = (P("grp", None, None), P("grp", None))
    out_specs = P("grp", "lag")

    def run(waveforms, pair_bin):
        body = local_by_frequency if fits_by_frequency(mesh, waveforms) else local
        return jax.shard_map(
            body, mesh=mesh, in_specs=in_specs, out_specs=out_specs, check_vma=False
        )(waveforms, pair_bin)

    return run
```

```python
import math

import jax
import jax.numpy as jnp
import ml_dtypes
import numpy as np
from jax import lax
from jax.experimental import pallas as pl
from jax.experimental.pallas import tpu as pltpu
from jax.sharding import PartitionSpec as P

NFFT = 2048
LAGS = 1024
HW = 32
BIN_DEV = 8


EPSILON = 1e-06


def with_halo(block, sides, width):
    for axis, dim in sides:
        count = lax.axis_size(axis)
        forward = [(i, i + 1) for i in range(count - 1)]
        backward = [(target, source) for source, target in forward]
        low = lax.ppermute(
            lax.slice_in_dim(block, block.shape[dim] - width, None, axis=dim), axis, forward
        )
        high = lax.ppermute(lax.slice_in_dim(block, 0, width, axis=dim), axis, backward)
        block = jnp.concatenate([low, block, high], axis=dim)
    return block


def forward_table(freq_start, freq_count):
    sample_index = jnp.arange(NFFT, dtype=jnp.int32)[:, None]
    bin_index = freq_start + jnp.arange(freq_count, dtype=jnp.int32)[None, :]
    phase = (sample_index * bin_index % NFFT).astype(jnp.float32) * (2.0 * math.pi / NFFT)
    return jnp.concatenate([jnp.cos(phase), -jnp.sin(phase)], axis=1)


def inverse_table(freq_start, freq_count):
    bin_index = freq_start + jnp.arange(freq_count, dtype=jnp.int32)
    shifted = jnp.arange(LAGS, dtype=jnp.int32) - LAGS // 2
    phase = (bin_index[:, None] * shifted[None, :] % NFFT).astype(jnp.float32) * (
        2.0 * math.pi / NFFT
    )
    weight = jnp.where(bin_index == 0, 1.0, 2.0).astype(jnp.float32)[:, None] / NFFT
    return jnp.concatenate([weight * jnp.cos(phase), -weight * jnp.sin(phase)], axis=0)


def window_band(freq_count):
    padded_index = jnp.arange(freq_count + 2 * HW, dtype=jnp.int32)[:, None]
    bin_index = jnp.arange(freq_count, dtype=jnp.int32)[None, :]
    inside = (padded_index >= bin_index) & (padded_index <= bin_index + 2 * HW)
    return inside.astype(jnp.float32)


def window_count(freq_start, freq_count, half_length):
    bin_index = freq_start + jnp.arange(freq_count, dtype=jnp.int32)
    upper = jnp.minimum(bin_index + HW, half_length - 1)
    lower = jnp.maximum(bin_index - HW, 0)
    return (upper - lower + 1).astype(jnp.float32)


def add_block(running, whitened, remote, column_start, keep_pairs, imag_sign, pair_bin):
    freq_count = whitened.shape[2] // 2
    row_count = whitened.shape[0]
    column_count = remote.shape[0]
    own_real = whitened[..., :freq_count]
    own_imag = whitened[..., freq_count:]
    far_real = remote[..., :freq_count]
    far_imag = remote[..., freq_count:]
    own_stack = jnp.concatenate([own_real, own_imag], axis=1)
    own_alt = jnp.concatenate([own_real, -own_imag], axis=1)
    far_stack = jnp.concatenate([far_real, far_imag], axis=1)
    far_alt = jnp.concatenate([far_imag, far_real], axis=1)
    real_sum = jnp.einsum("asf,bsf->abf", own_stack, far_stack, preferred_element_type=jnp.float32)
    imag_sum = (
        jnp.einsum("asf,bsf->abf", own_alt, far_alt, preferred_element_type=jnp.float32) * imag_sign
    )
    cross = jnp.concatenate([real_sum, imag_sum], axis=2).astype(jnp.bfloat16)
    cross = cross.reshape(row_count * column_count, 2 * freq_count)
    block_bins = lax.dynamic_slice_in_dim(pair_bin, column_start, column_count, 1)
    block_bins = jnp.where(keep_pairs, block_bins, -1).reshape(-1)
    onehot = (block_bins[None, :] == jnp.arange(running.shape[0], dtype=jnp.int32)[:, None]).astype(
        jnp.bfloat16
    )
    return running + jnp.dot(onehot, cross, preferred_element_type=jnp.float32)


def local(waveforms, pair_bin):
    station_count = waveforms.shape[0]
    segments = waveforms.shape[1]
    groups = lax.axis_size("grp")
    group_index = lax.axis_index("grp")
    half_length = NFFT // 2
    freq_count = half_length // lax.axis_size("lag")
    freq_start = lax.axis_index("lag") * freq_count
    spectra = jnp.dot(
        waveforms.reshape(station_count * segments, NFFT),
        forward_table(freq_start, freq_count),
        precision=lax.Precision.HIGHEST,
        preferred_element_type=jnp.float32,
    )
    spectra = spectra.reshape(station_count, segments, 2 * freq_count)
    real_part = spectra[..., :freq_count]
    imag_part = spectra[..., freq_count:]
    amplitude = jnp.sqrt(real_part * real_part + imag_part * imag_part)
    padded = with_halo(amplitude, (("lag", 2),), HW)
    smoothed = jnp.dot(
        padded.reshape(station_count * segments, freq_count + 2 * HW),
        window_band(freq_count),
        precision=lax.Precision.HIGHEST,
        preferred_element_type=jnp.float32,
    )
    smoothed = smoothed.reshape(station_count, segments, freq_count) / window_count(
        freq_start, freq_count, half_length
    )
    whitened = jnp.concatenate(
        [real_part / (smoothed + EPSILON), imag_part / (smoothed + EPSILON)], axis=2
    ).astype(jnp.bfloat16)
    bins_total = BIN_DEV * groups
    row_start = group_index * station_count
    initial = jnp.zeros((bins_total, 2 * freq_count), jnp.float32)
    local_rows = jnp.arange(station_count, dtype=jnp.int32)
    remote = lax.all_gather(whitened, "grp", axis=0, tiled=True)
    group_total = remote.shape[0] // station_count
    per_step = max((divisor for divisor in (4, 3, 2, 1) if group_total % divisor == 0))
    step_count = group_total // per_step
    block_width = per_step * station_count
    blocks = remote.reshape(step_count, block_width, remote.shape[1], remote.shape[2])

    def one_step(step_index, carried):
        column_block = lax.dynamic_index_in_dim(blocks, step_index, 0, keepdims=False)
        column_start = step_index * block_width
        column_index = column_start + jnp.arange(block_width, dtype=jnp.int32)
        keep_pairs = column_index[None, :] > (row_start + local_rows)[:, None]

        def compute(accumulated):
            return add_block(
                accumulated, whitened, column_block, column_start, keep_pairs, 1.0, pair_bin
            )

        return lax.cond(
            column_start + block_width > row_start,
            compute,
            lambda accumulated: accumulated,
            carried,
        )

    binned = lax.fori_loop(0, step_count, one_step, initial)
    inverse = inverse_table(freq_start, freq_count)
    owned_bins = lax.psum_scatter(binned, "grp", scatter_dimension=0, tiled=True)
    lag_partial = jnp.dot(
        owned_bins, inverse, precision=lax.Precision.HIGHEST, preferred_element_type=jnp.float32
    )
    return lax.psum_scatter(lag_partial, "lag", scatter_dimension=1, tiled=True)


LANES = 128
RADIX = 8
SPLIT = NFFT // RADIX
PACK = 16


def halves(table):
    wide = np.asarray(table, np.float32)
    high = wide.astype(ml_dtypes.bfloat16)
    return high, (wide - high.astype(np.float32)).astype(ml_dtypes.bfloat16)


def forward_constants():
    steps = SPLIT // 2
    sample = np.arange(SPLIT)
    angle = 2.0 * np.pi / SPLIT * (sample[:, None] * np.arange(steps)[None, :] % SPLIT)
    table = np.concatenate([np.cos(angle), np.sin(angle)], axis=1)
    small = np.zeros((3 * RADIX, SPLIT), np.float32)
    for r in range(RADIX):
        angle = 2.0 * np.pi / NFFT * (r * sample % NFFT)
        small[2 * r] = np.cos(angle)
        small[2 * r + 1] = np.sin(angle)
        bins = RADIX * np.arange(steps) + r
        upper = np.minimum(bins + HW, NFFT // 2 - 1)
        lower = np.maximum(bins - HW, 0)
        small[2 * RADIX + r, :steps] = 1.0 / (upper - lower + 1)
    return small, np.concatenate(halves(table), axis=1)


def inverse_constants(lag_count, groups):
    run = NFFT // 2 // (groups * lag_count)
    start = np.arange(groups * lag_count) * run
    pair, half, step = np.meshgrid(
        np.arange(2), np.arange(RADIX // 2), np.arange(run // RADIX), indexing="ij"
    )
    offset = (RADIX * step + RADIX // 2 * pair + half).reshape(2, PACK)
    bins = start[:, None, None] + offset[None]
    both = np.stack([bins, bins], axis=2)
    imaginary = np.stack([np.zeros_like(bins), np.ones_like(bins)], axis=2).reshape(-1)
    both = both.reshape(-1)
    angle = 2.0 * np.pi / NFFT * (both[:, None] * np.arange(LANES)[None, :] % NFFT)
    table = np.where(imaginary[:, None] == 1, -np.sin(angle), np.cos(angle))
    table_high, table_low = halves(table)
    lag_block = LAGS // lag_count
    weight = np.where(both == 0, 1.0, 2.0) / NFFT
    own, swapped = [], []
    for lag in range(lag_count):
        first = np.arange(lag_block // LANES) * LANES + lag * lag_block - LAGS // 2
        angle = 2.0 * np.pi / NFFT * (both[None, :] * first[:, None] % NFFT)
        own.append(weight * np.cos(angle))
        swapped.append(np.where(imaginary == 1, 1.0, -1.0) * weight * np.sin(angle))
    return (
        table_high,
        table_low,
        np.stack(own).astype(np.float32),
        np.stack(swapped).astype(np.float32),
    )


def split_float(value):
    high = value.astype(jnp.bfloat16)
    return high, (value - high.astype(jnp.float32)).astype(jnp.bfloat16)


def product(left, right):
    return jnp.dot(left, right, preferred_element_type=jnp.float32)


def product_transposed(left, right):
    return lax.dot_general(
        left, right, (((1,), (1,)), ((), ())), preferred_element_type=jnp.float32
    )


def whiten_kernel(
    bin_hbm, wave_hbm, small_hbm, table_hbm, out_ref,
    bin_ref, wave_ref, small_ref, table_ref, scratch, sems,
):
    rows = wave_ref.shape[0]
    owned = bin_ref.shape[0]
    segments = rows // owned
    targets = out_ref.shape[0]
    lag = lax.axis_index("lag")
    moves = (
        (small_hbm, small_ref),
        (wave_hbm.at[pl.ds(lag * rows, rows)], wave_ref),
        (table_hbm, table_ref),
        (bin_hbm.at[pl.ds(lag * owned, owned)], bin_ref),
    )
    copies = [
        pltpu.make_async_copy(source, target, sems.at[k])
        for k, (source, target) in enumerate(moves)
    ]
    for copy in copies:
        copy.start()
    steps = table_ref.shape[1] // 4
    reach = HW // RADIX
    row = lax.broadcasted_iota(jnp.int32, (steps, steps), 0)
    column = lax.broadcasted_iota(jnp.int32, (steps, steps), 1)
    near = jnp.where(jnp.abs(row - column) < reach, 1.0, 0.0).astype(jnp.bfloat16)
    for copy in copies:
        copy.wait()
    part = [wave_ref[:, k * SPLIT : (k + 1) * SPLIT] for k in range(RADIX)]
    sums = [part[k] + part[k + 4] for k in range(4)]
    gaps = [part[k] - part[k + 4] for k in range(4)]
    even, odd = sums[0] + sums[2], sums[1] + sums[3]
    even_gap, odd_gap = sums[0] - sums[2], sums[1] - sums[3]
    across, along = math.sqrt(0.5) * (gaps[1] - gaps[3]), math.sqrt(0.5) * (gaps[1] + gaps[3])
    folded = (
        (even + odd, None),
        (gaps[0] + across, -gaps[2] - along),
        (even_gap, -odd_gap),
        (gaps[0] - across, gaps[2] - along),
        (even - odd, None),
        (gaps[0] - across, along - gaps[2]),
        (even_gap, odd_gap),
        (gaps[0] + across, gaps[2] + along),
    )
    high, low = [], []
    for r, (first, second) in enumerate(folded):
        cosine, sine = small_ref[2 * r : 2 * r + 1, :], small_ref[2 * r + 1 : 2 * r + 2, :]
        turned_real, turned_imag = first * cosine, -first * sine
        if second is not None:
            turned_real = turned_real + second * sine
            turned_imag = turned_imag + second * cosine
        for turned in (turned_real, turned_imag):
            turned_high, turned_low = split_float(turned)
            high.append(turned_high)
            low.append(turned_low)
    high = jnp.concatenate(high, axis=0)
    low = jnp.concatenate(low, axis=0)
    table_high, table_low = table_ref[:, : 2 * steps], table_ref[:, 2 * steps :]
    value = product(high, table_high) + product(low, table_high) + product(high, table_low)
    spectra, amplitudes = [], []
    for r in range(RADIX):
        first = value[2 * r * rows : (2 * r + 1) * rows]
        second = value[(2 * r + 1) * rows : (2 * r + 2) * rows]
        real = first[:, :steps] + second[:, steps:]
        imag = second[:, :steps] - first[:, steps:]
        spectra.append((real, imag))
        amplitudes.append(jnp.sqrt(real * real + imag * imag))
    sums_high, sums_low = split_float(sum(amplitudes))
    common = product(sums_high, near) + product(sums_low, near)
    step = lax.broadcasted_iota(jnp.int32, (rows, steps), 1)
    for r, (real, imag) in enumerate(spectra):
        above = pltpu.roll(sum(amplitudes[: r + 1]), steps - reach, 1)
        above = jnp.where(step < steps - reach, above, 0.0)
        below = pltpu.roll(sum(amplitudes[r:]), reach, 1)
        below = jnp.where(step >= reach, below, 0.0)
        count = small_ref[2 * RADIX + r : 2 * RADIX + r + 1, :steps]
        scale = 1.0 / ((common + above + below) * count + EPSILON)
        scratch[0, r] = real * scale
        scratch[1, r] = imag * scale
    stations = bin_ref.shape[1]
    first_station = lax.axis_index("grp") * PACK + lag * owned
    turned = pltpu.roll(
        bin_ref[...].astype(jnp.float32), (stations - first_station) % stations, 1
    )
    following = jnp.concatenate(
        [
            pltpu.roll(turned[i : i + 1, :], stations - 1 - i, 1)[:, : stations // 2]
            for i in range(owned)
        ],
        axis=0,
    ).astype(jnp.bfloat16)
    width = LANES // targets
    chunk = lax.broadcasted_iota(jnp.int32, (PACK, LANES), 1) // width
    bits = []
    while 2 ** len(bits) < targets:
        odd_chunk = chunk // 2 ** len(bits) % 2
        bits.append(odd_chunk.astype(jnp.float32).astype(jnp.bfloat16) == jnp.bfloat16(1))
    for pair in range(2):
        tiles = []
        for half in range(RADIX // 2):
            for segment in range(segments):
                at = pl.ds(segment, owned, stride=segments)
                both = jnp.concatenate(
                    [scratch[k, RADIX // 2 * pair + half, at, :] for k in range(2)], axis=0
                )
                shift = width * (half * segments + segment)
                both = pltpu.roll(both, shift, 1) if shift else both
                tiles.append(both.astype(jnp.bfloat16))
        for bit, mask in enumerate(bits):
            tiles = [
                jnp.where(mask, tiles[(k + 2**bit) % targets], tiles[k]) for k in range(targets)
            ]
        for target in range(targets):
            out_ref[target, pair * PACK : (pair + 1) * PACK, :] = tiles[-target % targets]
    for target in range(targets):
        out_ref[target, 2 * PACK :, :] = following


def pair_kernel(data_ref, out_ref, spectra, cross, bins, total):
    groups = lax.axis_size("grp")
    stations = groups * PACK
    bin_count = total.shape[0]
    width = LANES // data_ref.shape[0]
    half = stations // 2
    shares = data_ref.shape[0] // groups
    owned = PACK // shares

    def gathered(group, first_row):
        return jnp.concatenate(
            [
                data_ref[group * shares + k, first_row : first_row + owned, :]
                for k in range(shares)
            ],
            axis=0,
        )

    for group in range(groups):
        for pair in range(2):
            for part in range(2):
                spectra[
                    pair, group * PACK : (group + 1) * PACK, part * LANES : (part + 1) * LANES
                ] = gathered(group, pair * PACK + part * owned)
    station = lax.broadcasted_iota(jnp.int32, (half, half), 0)
    column = lax.broadcasted_iota(jnp.int32, (half, half), 1)
    for group in range(groups // 2):
        following = jnp.concatenate(
            [gathered(group, 2 * PACK), gathered(group + groups // 2, 2 * PACK)], axis=1
        ).astype(jnp.float32)
        bins[group * PACK : (group + 1) * PACK, :] = pltpu.roll(
            following, group * PACK + 1, 1, stride=1, stride_axis=0
        )
    near, far = bins[:, :half], bins[:, half:]
    inner = jnp.where(column > station, near, jnp.where(column < station, far.T, -1.0))
    bins[:, half:] = jnp.where(column <= station, far, near.T)
    bins[:, :half] = inner

    def spread(value):
        return jnp.broadcast_to(value, (PACK, value.shape[1])).astype(jnp.bfloat16)

    def swap(value):
        return jnp.concatenate([value[:, LANES:], value[:, :LANES]], axis=1)

    def as_float(mask):
        return jnp.where(mask, 1.0, 0.0)

    lane = lax.broadcasted_iota(jnp.int32, (PACK, 2 * LANES), 1)
    row = lax.broadcasted_iota(jnp.int32, (PACK, 2 * LANES), 0)
    position = lax.axis_index("grp") * shares + lax.axis_index("lag")
    place = (lane % LANES // width - position + shares * groups) % (shares * groups)
    slot = place // (LANES // PACK) * width + lane % width
    sign = jnp.where(lane < LANES, -1.0, 1.0)
    keep = as_float(slot == row)
    keep_own = keep.astype(jnp.bfloat16)
    keep_turned = (keep * sign).astype(jnp.bfloat16)
    folded = as_float(slot % (PACK // 2) == row % (PACK // 2))
    fold_own = jnp.where(row < PACK // 2, folded, 0.0).astype(jnp.bfloat16)
    fold_turned = jnp.where(row < PACK // 2, 0.0, -sign * folded).astype(jnp.bfloat16)
    first_bins = as_float(slot[:1] < PACK // 2).astype(jnp.bfloat16)
    last_bins = as_float(slot[:1] >= PACK // 2).astype(jnp.bfloat16)
    eight = PACK // 2
    for chunk in range(groups // 2):
        start = chunk * PACK
        for pair in range(2):
            own = spectra[pair, start : start + PACK, :].astype(jnp.float32)
            other = spectra[pair, half + start : half + start + PACK, :].astype(jnp.float32)
            upper, lower = [], []
            for i in range(PACK):
                value = spread(own[i : i + 1, :])
                upper += [value * keep_own, swap(value) * keep_turned]
                value = spread(other[i : i + 1, :])
                lower.append(value * fold_own + swap(value) * fold_turned)
            first = product_transposed(jnp.concatenate(upper, axis=0), spectra[pair])
            second_half = spectra[pair, half:, :]
            second = product_transposed(
                jnp.concatenate(lower, axis=0),
                jnp.concatenate([second_half * first_bins, second_half * last_bins], axis=0),
            )
            rows = slice(pair * 2 * PACK, (pair + 1) * 2 * PACK)
            for i in range(PACK):
                mine = first[i * 2 * PACK : (i + 1) * 2 * PACK]
                theirs = second[i * PACK : (i + 1) * PACK]
                theirs = jnp.concatenate(
                    [
                        theirs[:eight, :half],
                        theirs[:eight, half:],
                        theirs[eight:, :half],
                        theirs[eight:, half:],
                    ],
                    axis=0,
                )
                inner = jnp.where(column[:1] > start + i, mine[:, :half], theirs)
                at = i * stations
                cross[chunk, rows, at : at + half] = inner.astype(jnp.bfloat16)
                cross[chunk, rows, at + half : at + stations] = mine[:, half:].astype(jnp.bfloat16)
    wanted = lax.broadcasted_iota(jnp.int32, (bin_count, stations), 0).astype(jnp.float32)
    wanted = wanted.astype(jnp.bfloat16)
    one, zero = jnp.bfloat16(1), jnp.bfloat16(0)
    for chunk in range(groups // 2):
        chunk_bins = bins[chunk * PACK : (chunk + 1) * PACK, :]
        hot = []
        for i in range(PACK):
            bin_row = spread(chunk_bins[i : i + 1, :])
            hot.append(
                jnp.concatenate(
                    [
                        jnp.where(bin_row == wanted[k : k + PACK], one, zero)
                        for k in range(0, bin_count, PACK)
                    ],
                    axis=0,
                )
            )
        added = product_transposed(jnp.concatenate(hot, axis=1), cross[chunk])
        total[...] = total[...] + added if chunk else added
    copies = out_ref.shape[0] // groups
    middle = BIN_DEV // 2
    for group in range(groups):
        upper = total[group * BIN_DEV : group * BIN_DEV + middle, :]
        lower = total[group * BIN_DEV + middle : (group + 1) * BIN_DEV, :]
        value = jnp.concatenate([upper, lower], axis=1)
        for k in range(copies):
            out_ref[group * copies + k] = value


def lag_kernel(data_ref, high_ref, low_ref, own_ref, swapped_ref, out_ref):
    lag = lax.axis_index("lag")
    sources = data_ref.shape[0]
    owned, blocks = out_ref.shape[0], out_ref.shape[1] // LANES
    lane = lax.broadcasted_iota(jnp.int32, (owned, LANES), 1)
    is_real = lane % (2 * PACK) < PACK
    is_first = lane[: owned // 2] < LANES // 2
    turned = [[] for _ in range(blocks)]
    for tile in range(sources // 2):
        first, second = data_ref[2 * tile], data_ref[2 * tile + 1]
        value = jnp.concatenate(
            [
                jnp.where(is_first, first, pltpu.roll(second, LANES // 2, 1)),
                jnp.where(is_first, pltpu.roll(first, LANES // 2, 1), second),
            ],
            axis=0,
        )
        partner = jnp.where(
            is_real, pltpu.roll(value, LANES - PACK, 1), pltpu.roll(value, PACK, 1)
        )
        at = slice(tile * LANES, (tile + 1) * LANES)
        for block in range(blocks):
            turned[block].append(
                value * own_ref[lag, block : block + 1, at]
                + partner * swapped_ref[lag, block : block + 1, at]
            )
    left = jnp.concatenate([jnp.concatenate(row, axis=1) for row in turned], axis=0)
    left_high, left_low = split_float(left)
    rows = blocks * owned
    value = product(
        jnp.concatenate([left_high, left_low], axis=0),
        jnp.concatenate([high_ref[...], low_ref[...]], axis=1),
    )
    value = value[:rows, :LANES] + value[:rows, LANES:] + value[rows:, :LANES]
    for block in range(blocks):
        out_ref[:, block * LANES : (block + 1) * LANES] = value[block * owned : (block + 1) * owned]


def call(kernel, arrays, spaces, out_shape, scratch=()):
    arrays = [
        pltpu.with_memory_space_constraint(array, space) if space is pltpu.HBM else array
        for array, space in zip(arrays, spaces)
    ]
    return pl.pallas_call(
        kernel,
        in_specs=[pl.BlockSpec(memory_space=space) for space in spaces],
        out_specs=pl.BlockSpec(memory_space=pltpu.VMEM),
        out_shape=out_shape,
        scratch_shapes=list(scratch),
        compiler_params=pltpu.CompilerParams(vmem_limit_bytes=48 << 20),
    )(*arrays)


def local_by_frequency(waveforms, pair_bin):
    station_count, segments, _ = waveforms.shape
    groups = lax.axis_size("grp")
    lag_count = lax.axis_size("lag")
    stations = station_count * groups
    bin_count = BIN_DEV * groups
    rows = waveforms.reshape(station_count * segments, NFFT)
    small, table = [jnp.asarray(t) for t in forward_constants()]
    owned = station_count // lag_count
    whitened = call(
        whiten_kernel,
        [pair_bin, rows, small, table],
        [pltpu.HBM] * 4,
        jax.ShapeDtypeStruct((groups * lag_count, 2 * PACK + owned, LANES), jnp.bfloat16),
        [
            pltpu.VMEM((owned, stations), jnp.int32),
            pltpu.VMEM((owned * segments, NFFT), jnp.float32),
            pltpu.VMEM(small.shape, jnp.float32),
            pltpu.VMEM(table.shape, jnp.bfloat16),
            pltpu.VMEM((2, RADIX, owned * segments, LANES), jnp.float32),
            pltpu.SemaphoreType.DMA((4,)),
        ],
    )
    received = lax.all_to_all(whitened, ("grp", "lag"), 0, 0, tiled=True)
    outgoing = call(
        pair_kernel,
        [received],
        [pltpu.VMEM],
        jax.ShapeDtypeStruct((groups * lag_count, BIN_DEV // 2, LANES), jnp.float32),
        [
            pltpu.VMEM((2, stations, 2 * LANES), jnp.bfloat16),
            pltpu.VMEM((groups // 2, 4 * PACK, PACK * stations), jnp.bfloat16),
            pltpu.VMEM((stations // 2, stations), jnp.float32),
            pltpu.VMEM((bin_count, 4 * PACK), jnp.float32),
        ],
    )
    owned = lax.all_to_all(outgoing, ("grp", "lag"), 0, 0, tiled=True)
    high, low, own, swapped = [
        jnp.asarray(t) for t in inverse_constants(lag_count, groups)
    ]
    return call(
        lag_kernel,
        [owned, high, low, own, swapped],
        [pltpu.VMEM] * 5,
        jax.ShapeDtypeStruct((BIN_DEV, LAGS // lag_count), jnp.float32),
    )


def fits_by_frequency(mesh, waveforms):
    groups, lag_count = mesh.shape["grp"], mesh.shape["lag"]
    stations, segments, _ = waveforms.shape
    return (
        lag_count == 2
        and stations == groups * PACK == 2 * LANES
        and segments * PACK == LANES
        and groups * lag_count * 2 * PACK == NFFT // 2 == RADIX * LANES
        and groups * BIN_DEV <= 256
    )


def solution(mesh):
    in_specs = (P("grp", None, None), P("grp", None))
    out_specs = P("grp", "lag")

    def run(waveforms, pair_bin):
        body = local_by_frequency if fits_by_frequency(mesh, waveforms) else local
        return jax.shard_map(
            body, mesh=mesh, in_specs=in_specs, out_specs=out_specs, check_vma=False
        )(waveforms, pair_bin)

    return run
```
